32 devices in a mesh: spot: 4 (over x, core), cell: 8 (over z, y).
Axes of the slice: x: 2, y: 2, z: 4, core: 2. Of those that a mesh axis runs over, the one named last changes fastest.
Arguments:
- logits: float32 [4096, 4096], P('cell', 'spot'), may hold values from -6 to 6
- expression: float32 [4096, 2048], P('cell', 'spot'), may hold values from 0.05 to 5
- spatial: float32 [2048, 4096], P('cell', 'spot'), may hold values from 0.05 to 5
- density: float32 [4096], P('spot'), may hold values from 0.2 to 5
- slide_ids: int32 [4096], replicated, may hold values from 0 to 2, as said below
- spot_valid: int32 [4096], replicated, may hold values 0 or 1
- neighbours: int32 [4096, 6], P('spot'), may hold values from -1 to 4095, as said below
Outputs:
- gene_loss: float32 [], replicated
- spot_loss: float32 [], replicated
- density_loss: float32 [], replicated
- grad_logits: float32 [4096, 4096], P('cell', 'spot')
- grad_expr: float32 [4096, 2048], P('cell', 'spot')
- rms_weights: float32 [], replicated
- rms_pred: float32 [], replicated
- rms_smooth: float32 [], replicated
The draws below stay inside these ranges and needn't reach their ends.
Inputs may be any that keep to these rules, and one draw needn't show every extreme that they name: `slide_ids`: slide ids never fall along the spots, and each of the 3 slides holds whole grid rows of 64 spots. `neighbours`: spots lie row by row on a hexagonal grid with 64 spots a row, odd rows shifted; every listed neighbour is an adjacent grid spot, at most 65 away in index.
All inputs are finite; a program needn't handle non-finite values.
Results may differ from the reference program's by a relative error of at most 0.0003.
Values sent between devices are 32-bit elements; how exact they have to be, the bound alone decides.
No kernel may reach another device: no remote copies, remote signals or barrier semaphores. Data moves between devices by JAX's collectives and lax.ppermute only.
A program may use at most 128 MiB of HBM per device.

```python
import math
import jax
import jax.numpy as jnp
from jax import lax

GENES = 2048
ROW = 64
SLIDES = 3
CELLS = 4096
SPOTS = 4096


def draw_slide_ids(key, part):
    grid_rows = SPOTS // ROW
    first_cut = jax.random.randint(jax.random.fold_in(key, 11), (), grid_rows // 4, grid_rows // 2)
    second_cut = jax.random.randint(jax.random.fold_in(key, 12), (), grid_rows // 2 + 1, 3 * grid_rows // 4 + 1)
    spot_row = jnp.arange(SPOTS, dtype=jnp.int32) // ROW
    return ((spot_row >= first_cut).astype(jnp.int32) + (spot_row >= second_cut).astype(jnp.int32)).astype(jnp.int32)


def draw_neighbours(key, part):
    grid_rows = SPOTS // ROW
    spot_index = jnp.arange(SPOTS, dtype=jnp.int32)
    spot_row = spot_index // ROW
    spot_col = spot_index % ROW
    row_step = jnp.array([0, 0, -1, -1, 1, 1], dtype=jnp.int32)
    even_step = jnp.array([-1, 1, -1, 0, -1, 0], dtype=jnp.int32)
    odd_step = jnp.array([-1, 1, 0, 1, 0, 1], dtype=jnp.int32)
    col_step = jnp.where((spot_row % 2)[:, None] == 1, odd_step[None, :], even_step[None, :])
    other_row = spot_row[:, None] + row_step[None, :]
    other_col = spot_col[:, None] + col_step
    inside = (other_row >= 0) & (other_row < grid_rows) & (other_col >= 0) & (other_col < ROW)
    kept = jax.random.randint(jax.random.fold_in(key, 21), (SPOTS, 6), 0, 6) != 0
    return jnp.where(inside & kept, other_row * ROW + other_col, -1).astype(jnp.int32)


def with_ends(drawn, stream_key, least, top_value):
    spot = [jax.random.randint(jax.random.fold_in(stream_key, axis), (), 0, length) for axis, length in enumerate(drawn.shape)]
    widest = drawn.shape.index(max(drawn.shape))
    next_to = spot[:widest] + [(spot[widest] + 1) % drawn.shape[widest]] + spot[widest + 1:]
    return drawn.at[tuple(spot)].set(least).at[tuple(next_to)].set(top_value)


def levels(rng, extent, split, low, high):
    loudness, own = 1.0, jax.random.fold_in(rng, 6)
    for position, blocks in split:
        draws = jnp.exp(jax.random.uniform(jax.random.fold_in(own, position), (blocks,), jnp.float32, low / len(split), high / len(split)))
        loudness = loudness * jnp.repeat(draws, extent[position] // blocks).reshape([-1 if axis == position else 1 for axis in range(len(extent))])
    return loudness


def bell_draw(stream_key, dims, width, reach, cuts=(), kind=jnp.bfloat16):
    gain = levels(stream_key, dims, cuts, -0.22, 0.18) if cuts else 1.0
    result = jax.random.normal(stream_key, dims, jnp.float32) * width * gain
    return jnp.minimum(jnp.maximum(result, -reach), reach).astype(kind)


def setup_inputs(seed: int = 0) -> dict:
    seeds = jax.random.split(jax.random.key(seed), 8)
    logits = bell_draw(seeds[0], (CELLS, SPOTS), 1.0, 6.0, ((0, 8), (1, 4)), jnp.float32)
    expression = jnp.clip(jnp.exp(math.log(5.0) - 4.6051702 * jax.random.uniform(seeds[1], (CELLS, GENES), jnp.float32) ** levels(seeds[1], (CELLS, GENES), ((0, 8), (1, 4)), -0.2, 0.2)), 0.05, 5.0)
    spatial = jnp.clip(jnp.exp(math.log(5.0) - 4.6051702 * jax.random.uniform(seeds[2], (GENES, SPOTS), jnp.float32) ** levels(seeds[2], (GENES, SPOTS), ((0, 8), (1, 4)), -0.2, 0.2)), 0.05, 5.0)
    density = jnp.clip(jnp.exp(math.log(5.0) - 3.218876 * jax.random.uniform(seeds[3], (SPOTS,), jnp.float32) ** levels(seeds[3], (SPOTS,), ((0, 4),), -0.2, 0.2)), 0.2, 5.0)
    slide_ids = draw_slide_ids(jax.random.fold_in(seeds[7], 71), 0)
    spot_valid = with_ends((jax.random.randint(seeds[5], (SPOTS,), 0, 8) < 7).astype(jnp.int32), jax.random.fold_in(seeds[5], 1), 0, 1)
    neighbours = draw_neighbours(jax.random.fold_in(seeds[7], 71), 0)
    return dict(logits=logits, expression=expression, spatial=spatial, density=density, slide_ids=slide_ids, spot_valid=spot_valid, neighbours=neighbours)


epsilon = 1e-06
highest = lax.Precision.HIGHEST

def cosine_parts(smoothed, spatial, weight, over_dim):
    inner_sum = lax.optimization_barrier(jnp.sum(weight * smoothed * spatial, axis=over_dim))
    own_sq = lax.optimization_barrier(jnp.sum(weight * smoothed * smoothed, axis=over_dim))
    target_sq = lax.optimization_barrier(jnp.sum(weight * spatial * spatial, axis=over_dim))
    return inner_sum * lax.rsqrt((own_sq + epsilon) * (target_sq + epsilon))

def reference(logits, expression, spatial, density, slide_ids, spot_valid, neighbours):
    block_size = min(512, SPOTS)
    blocks = SPOTS // block_size
    valid_f = spot_valid.astype(jnp.float32)
    nvalid = jnp.sum(valid_f)
    clamped = jnp.maximum(neighbours, 0).astype(jnp.int32)
    linked = ((neighbours >= 0) & (spot_valid[clamped] == 1) & (slide_ids[clamped] == slide_ids[:, None])).astype(jnp.float32)
    counts = 1.0 + lax.optimization_barrier(jnp.sum(linked, axis=1))
    members = (slide_ids[:, None] == jnp.arange(SLIDES, dtype=jnp.int32)[None, :]).astype(jnp.float32)
    target_tot = lax.optimization_barrier(jnp.sum(members * (valid_f * density)[:, None], axis=0))
    target = density / lax.optimization_barrier(jnp.sum(members * target_tot[None, :], axis=1))

    def forward(logit_all, expr_all):
        logit_tiles = logit_all.reshape(CELLS, blocks, block_size).transpose(1, 0, 2)
        mask_tiles = valid_f.reshape(blocks, block_size)

        def column_block(inputs):
            logit_tile, mask_tile = inputs
            column_max = lax.optimization_barrier(jnp.max(logit_tile, axis=0))
            raised = jnp.exp(logit_tile - column_max)
            mapping = raised / lax.optimization_barrier(jnp.sum(raised, axis=0))
            partial_value = jnp.dot(expr_all.T, mapping, precision=highest)
            return (partial_value, lax.optimization_barrier(jnp.sum(mapping * mapping, axis=0)) * mask_tile)
        partials, squares = lax.map(jax.checkpoint(column_block), (logit_tiles, mask_tiles))
        predicted = partials.transpose(1, 0, 2).reshape(GENES, SPOTS)
        summed = predicted
        for k in range(6):
            summed = summed + linked[:, k][None, :] * predicted[:, clamped[:, k]]
        smoothed = summed / counts[None, :]
        cos_gene = cosine_parts(smoothed, spatial, valid_f[None, :], 1)
        cos_spot = cosine_parts(smoothed, spatial, 1.0, 0)
        row_sums = lax.optimization_barrier(jnp.sum(predicted, axis=0))
        row_tot = lax.optimization_barrier(jnp.sum(members * (valid_f * row_sums)[:, None], axis=0))
        predicted_share = row_sums / lax.optimization_barrier(jnp.sum(members * row_tot[None, :], axis=1))
        density_loss = jnp.sum(valid_f * target * (jnp.log(target) - jnp.log(predicted_share)))
        gene_loss = 1.0 - jnp.mean(cos_gene)
        spot_loss = 1.0 - jnp.sum(valid_f * cos_spot) / nvalid
        objective = CELLS * (GENES * gene_loss + SPOTS * spot_loss + SPOTS * density_loss)
        rms_weights = CELLS * jnp.sqrt(jnp.sum(squares) / (CELLS * nvalid))
        rms_pred = jnp.sqrt(jnp.sum(valid_f[None, :] * predicted * predicted) / (GENES * nvalid))
        rms_smooth = jnp.sqrt(jnp.sum(valid_f[None, :] * smoothed * smoothed) / (GENES * nvalid))
        return (objective, (gene_loss, spot_loss, density_loss, rms_weights, rms_pred, rms_smooth))
    objective, pullback, extras = jax.vjp(forward, logits, expression, has_aux=True)
    grad_logits, grad_expr = pullback(jnp.ones_like(objective))
    return (extras[0], extras[1], extras[2], grad_logits, grad_expr, extras[3], extras[4], extras[5])
```

```python
import jax
import jax.numpy as jnp
from jax import lax
from jax.sharding import PartitionSpec as P

GENES = 2048
ROW = 64
SLIDES = 3
SIDE = 2 * ROW
OFFSETS = (-ROW - 1, -ROW, -ROW + 1, -1, 1, ROW - 1, ROW, ROW + 1)

epsilon = 1e-06
highest = lax.Precision.HIGHEST


def apart(*values):
    return lax.optimization_barrier(values)


def bits_of(count):
    return [1 << b for b in range(count.bit_length() - 1)]


def all_sum(value, axis, bits):
    size = lax.axis_size(axis)
    for bit in bits:
        value = value + lax.ppermute(value, axis, [(i, i ^ bit) for i in range(size)])
    return value


def is_one_of(index, wanted):
    hit = index == wanted[0]
    for other in wanted[1:]:
        hit = hit | (index == other)
    return hit


def choose(index, options):
    options = [o for o in options if o[1]]
    chosen = options[0][0]
    for value, wanted in options[1:]:
        chosen = jnp.where(is_one_of(index, wanted), value, chosen)
    return chosen


def shards(logits, expression, spatial, density, slide_ids, spot_valid, neighbours):
    cells, spots = logits.shape
    genes = spatial.shape[0]
    gene_cols = expression.shape[1]
    n_spot, n_cell = lax.axis_size("spot"), lax.axis_size("cell")
    total_cells, total_spots = cells * n_cell, spots * n_spot
    lines, peers = n_spot, n_cell // n_spot
    few_peers = peers <= 2
    s = lax.axis_index("spot")
    k = lax.axis_index("cell")
    z, y = k // peers, k % peers
    offset = s * spots

    def turn(value, d):
        pairs = [(i, (i // peers) * peers + (i % peers + d) % peers) for i in range(n_cell)]
        return lax.ppermute(value, "cell", pairs)

    held = {0: expression}
    for bit in reversed(bits_of(n_spot)):
        pairs = [(i, i ^ bit) for i in range(n_spot)]
        held.update({m ^ bit: lax.ppermute(v, "spot", pairs) for m, v in list(held.items())})
    genes_all = jnp.concatenate(
        [choose(s, [(held[m], [i for i in range(n_spot) if i ^ m == j]) for m in held]) for j in range(n_spot)],
        axis=1,
    )
    (genes_all,) = apart(genes_all)

    def gene_block(block):
        return lax.dynamic_slice_in_dim(genes_all, block * genes, genes, axis=1)

    local_max = jnp.max(logits, axis=0)
    raised = jnp.exp(logits - local_max)
    local_sum = jnp.sum(raised, axis=0)
    (raised,) = apart(raised)
    own_pair = jnp.stack([local_max, local_sum])
    turned = [own_pair] + [turn(own_pair, d) for d in range(1, peers)]

    def joined(a, b):
        top = jnp.maximum(a[0], b[0])
        return jnp.stack([top, a[1] * jnp.exp(a[0] - top) + b[1] * jnp.exp(b[0] - top)])

    both = turned[0]
    for other in turned[1:]:
        both = joined(both, other)
    for bit in bits_of(lines):
        both = joined(both, lax.ppermute(both, "cell", [(i, i ^ (bit * peers)) for i in range(n_cell)]))
    scales = [jnp.exp(t[0] - both[0]) / both[1] for t in turned]
    mapping = raised * scales[0]

    frame = spots + 2 * SIDE
    valid_all = spot_valid.astype(jnp.float32)
    nvalid = jnp.sum(valid_all)
    reach = SIDE + ROW + 1
    wide_valid = lax.dynamic_slice_in_dim(jnp.pad(valid_all, reach), offset, spots + 2 * reach)
    wide_slide = lax.dynamic_slice_in_dim(
        jnp.pad(slide_ids, reach, constant_values=-1), offset, spots + 2 * reach
    )
    up_spot = [(i, i + 1) for i in range(n_spot - 1)]
    down_spot = [(i + 1, i) for i in range(n_spot - 1)]

    def framed(tile):
        before = lax.ppermute(tile[:, -SIDE:], "spot", up_spot)
        after = lax.ppermute(tile[:, :SIDE], "spot", down_spot)
        return jnp.concatenate([before, tile, after], axis=1)

    lists = framed(neighbours.T)
    spatial_wide = framed(spatial)
    spot_index = offset - SIDE + jnp.arange(frame, dtype=jnp.int32)
    inner = ROW + 1
    slide_frame = wide_slide[inner : inner + frame]
    valid_frame = wide_valid[inner : inner + frame]
    links = []
    for o in OFFSETS:
        listed = jnp.sum(((lists >= 0) & (lists == spot_index + o)).astype(jnp.float32), axis=0)
        there = wide_valid[inner + o : inner + o + frame] == 1.0
        same = wide_slide[inner + o : inner + o + frame] == slide_frame
        links.append(jnp.where(there & same, listed, 0.0))
    links = jnp.stack(links)
    counts = 1.0 + jnp.sum(links, axis=0)
    links, counts = apart(links, counts)
    valid_here = valid_frame[SIDE : SIDE + spots]
    slide_here = slide_frame[SIDE : SIDE + spots]
    members = (slide_here[None, :] == jnp.arange(SLIDES, dtype=jnp.int32)[:, None]).astype(jnp.float32)

    order = [sorted(range(lines), key=lambda t: (-abs(t - a), abs(2 * t - lines + 1))) for a in range(lines)]

    def part(block):
        return lax.dot_general(gene_block(block), raised, (((0,), (0,)), ((), ())), precision=highest)

    def line_pairs(pairs):
        return [(a * peers + c, b * peers + c) for a, b in pairs for c in range(peers)]

    def along(up_value, up_from, down_value, down_from):
        up_pairs = [(a, a + 1) for a in up_from]
        down_pairs = [(a, a - 1) for a in down_from]
        targets = {b for _, b in up_pairs} & {b for _, b in down_pairs}
        if targets or set(up_from) & set(down_from):
            return (
                lax.ppermute(up_value, "cell", line_pairs(up_pairs)),
                lax.ppermute(down_value, "cell", line_pairs(down_pairs)),
            )
        value = choose(z, [(up_value, list(up_from)), (down_value, list(down_from))])
        moved = lax.ppermute(value, "cell", line_pairs(up_pairs + down_pairs))
        return moved, moved

    if few_peers:
        units = []
        for u in range(lines):
            to = jnp.array([order[a][u] for a in range(lines)], jnp.int32)[z]
            sent = [turn(part(to * peers + (y + d) % peers), d) for d in range(1, peers)]
            unit = part(to * peers + y) * scales[0]
            for value, scale in zip(sent, scales[1:]):
                unit = unit + value * scale
            units.append(unit)

        def unit_for(target):
            wanted = [[] for _ in range(lines)]
            for a in range(lines):
                if 0 <= target(a) < lines:
                    wanted[order[a].index(target(a))].append(a)
            return choose(z, list(zip(units, wanted)))

        got_up = got_down = None
        for p in range(lines - 1, 0, -1):
            up_value, down_value = unit_for(lambda a: a + p), unit_for(lambda a: a - p)
            if got_up is not None:
                up_value, down_value = up_value + got_up, down_value + got_down
            got_up, got_down = along(up_value, range(0, lines - p), down_value, range(p, lines))
        predicted = unit_for(lambda a: a)
        if got_up is not None:
            predicted = predicted + got_up + got_down
    else:
        whole = lax.dot_general(genes_all, mapping, (((0,), (0,)), ((), ())), precision=highest)
        predicted = lax.psum_scatter(whole, "cell", scatter_dimension=0, tiled=True)

    wide = framed(predicted)

    def shifted(value, o):
        return jnp.pad(value, ((0, 0), (ROW + 1, ROW + 1)))[:, ROW + 1 + o : ROW + 1 + o + frame]

    summed = wide
    for i, o in enumerate(OFFSETS):
        summed = summed + links[i] * shifted(wide, o)
    smoothed_wide = summed / counts
    wide, smoothed_wide, spatial_wide = apart(wide, smoothed_wide, spatial_wide)
    spot_sums = jnp.stack(
        [
            jnp.sum(smoothed_wide * spatial_wide, axis=0),
            jnp.sum(smoothed_wide * smoothed_wide, axis=0),
            jnp.sum(spatial_wide * spatial_wide, axis=0),
            jnp.sum(wide, axis=0),
        ]
    )
    here = slice(SIDE, SIDE + spots)
    smoothed, weighted = smoothed_wide[:, here], valid_here[None, :]
    own_rows = spot_sums[3, here]
    gene_sums = jnp.concatenate(
        [
            jnp.sum(weighted * smoothed * spatial, axis=1),
            jnp.sum(weighted * smoothed * smoothed, axis=1),
            jnp.sum(weighted * spatial * spatial, axis=1),
            jnp.sum(members * (valid_here * own_rows)[None, :], axis=1),
            jnp.sum(members * (valid_here * density)[None, :], axis=1),
        ]
    )
    gene_sums = all_sum(gene_sums, "spot", bits_of(n_spot))
    spot_sums = all_sum(spot_sums, "cell", bits_of(n_cell))
    gene_inner, gene_own, gene_target = (gene_sums[i * genes : (i + 1) * genes] for i in range(3))
    row_tot = all_sum(gene_sums[3 * genes : 3 * genes + SLIDES], "cell", bits_of(n_cell))
    target_tot = gene_sums[3 * genes + SLIDES :]
    spot_inner, spot_own, spot_target, row_sums = (spot_sums[i] for i in range(4))
    row_sums = row_sums[here]
    gene_scale = lax.rsqrt((gene_own + epsilon) * (gene_target + epsilon))
    spot_scale = lax.rsqrt((spot_own + epsilon) * (spot_target + epsilon))
    cos_gene = gene_inner * gene_scale
    cos_spot = (spot_inner * spot_scale)[here]
    target = density / jnp.sum(members * target_tot[:, None], axis=0)
    slide_rows = jnp.sum(members * row_tot[:, None], axis=0)
    kl_terms = valid_here * target * (jnp.log(target) - jnp.log(row_sums / slide_rows))
    level = total_cells * total_spots * valid_here * (1.0 / slide_rows - target / row_sums)

    by_gene = total_cells * gene_scale
    by_spot = total_cells * total_spots / nvalid * spot_scale
    spread_in = (
        -valid_frame
        / counts
        * (
            (spatial_wide - (gene_inner / (gene_own + epsilon))[:, None] * smoothed_wide) * by_gene[:, None]
            + (spatial_wide - (spot_inner / (spot_own + epsilon))[None, :] * smoothed_wide) * by_spot[None, :]
        )
    )
    (spread_in,) = apart(spread_in)
    spread = spread_in
    for i, o in enumerate(OFFSETS):
        spread = spread + shifted(links[i] * spread_in, -o)
    grad_pred = spread[:, here]
    (grad_pred,) = apart(grad_pred)

    column_dot = all_sum(jnp.sum(predicted * grad_pred, axis=0), "cell", bits_of(n_cell))
    column_dot = column_dot + level * row_sums

    (mapping,) = apart(mapping)
    grad_map = jnp.sum(genes_all, axis=1)[:, None] * level[None, :]
    share = jnp.sum(mapping * level[None, :], axis=1)
    if few_peers:
        far = [sorted((t for t in range(lines)), key=lambda t: (abs(t - a), t)) for a in range(lines)]
        ups, downs = [grad_pred], [grad_pred]
        for p in range(1, lines):
            up, down = along(ups[-1], range(p - 1, lines - 1), downs[-1], range(1, lines - p + 1))
            ups.append(up)
            downs.append(down)
        slots = []
        for u in range(lines):
            options = [(grad_pred, [])] + [(v, []) for v in ups[1:]] + [(v, []) for v in downs[1:]]
            for a in range(lines):
                t = far[a][u]
                at = 0 if t == a else (a - t if t < a else lines - 1 + t - a)
                options[at][1].append(a)
            slots.append(choose(z, options))

        kept = [None] * peers
        for u in range(lines):
            to = jnp.array([far[a][u] for a in range(lines)], jnp.int32)[z]
            blocks = [slots[u]] + [turn(slots[u], d) for d in range(1, peers)]
            for d, block in enumerate(blocks):
                names = to * peers + (y - d) % peers
                grad_map = grad_map + jnp.dot(gene_block(names), block, precision=highest)
                wide_grad = lax.dot_general(mapping, block, (((1,), (1,)), ((), ())), precision=highest)
                wide_grad = wide_grad + share[:, None]
                for bit in bits_of(n_spot):
                    pairs = []
                    for i in range(n_cell):
                        t = far[i // peers][u]
                        for j in range(n_spot):
                            if (j ^ t) & (2 * bit - 1) == bit:
                                pairs.append((j * n_cell + i, (j ^ bit) * n_cell + i))
                    wide_grad = wide_grad + lax.ppermute(wide_grad, ("spot", "cell"), pairs)
                mine = s == to
                kept[d] = wide_grad if kept[d] is None else jnp.where(mine, wide_grad, kept[d])
        grad_expr = jnp.zeros((cells, gene_cols), jnp.float32)
        for d in range(peers):
            grad_expr = lax.dynamic_update_slice_in_dim(grad_expr, kept[d], ((y - d) % peers) * genes, axis=1)
    else:
        rows = lax.all_gather(grad_pred, "cell", axis=0, tiled=True)
        grad_map = grad_map + jnp.dot(genes_all, rows, precision=highest)
        wide_grad = lax.dot_general(mapping, rows, (((1,), (1,)), ((), ())), precision=highest)
        grad_expr = lax.psum_scatter(wide_grad + share[:, None], "spot", scatter_dimension=1, tiled=True)
    grad_logits = mapping * (grad_map - column_dot[None, :])

    first_spot = (s == 0).astype(jnp.float32)
    first_cell = (k == 0).astype(jnp.float32)
    totals = jnp.stack(
        [
            first_spot * jnp.sum(cos_gene),
            first_cell * jnp.sum(valid_here * cos_spot),
            first_cell * jnp.sum(kl_terms),
            jnp.sum(mapping * mapping * weighted),
            jnp.sum(weighted * predicted * predicted),
            jnp.sum(weighted * smoothed * smoothed),
        ]
    )
    totals = all_sum(totals, "spot", bits_of(n_spot))
    totals = all_sum(totals, "cell", bits_of(n_cell))
    gene_loss = 1.0 - totals[0] / GENES
    spot_loss = 1.0 - totals[1] / nvalid
    density_loss = totals[2]
    rms_weights = total_cells * jnp.sqrt(totals[3] / (total_cells * nvalid))
    rms_pred = jnp.sqrt(totals[4] / (GENES * nvalid))
    rms_smooth = jnp.sqrt(totals[5] / (GENES * nvalid))
    return (gene_loss, spot_loss, density_loss, grad_logits, grad_expr, rms_weights, rms_pred, rms_smooth)


def solution(mesh):
    placed = (
        P("cell", "spot"),
        P("cell", "spot"),
        P("cell", "spot"),
        P("spot"),
        P(),
        P(),
        P("spot", None),
    )
    return jax.shard_map(
        shards,
        mesh=mesh,
        in_specs=placed,
        out_specs=(P(), P(), P(), P("cell", "spot"), P("cell", "spot"), P(), P(), P()),
        check_vma=False,
    )
```

```python
import jax
import jax.numpy as jnp
from jax import lax
from jax.sharding import PartitionSpec as P

GENES = 2048
ROW = 64
SLIDES = 3
SIDE = 2 * ROW
OFFSETS = (-ROW - 1, -ROW, -ROW + 1, -1, 1, ROW - 1, ROW, ROW + 1)

epsilon = 1e-06
highest = lax.Precision.HIGHEST


def apart(*values):
    return lax.optimization_barrier(values)


def bits_of(count):
    return [1 << b for b in range(count.bit_length() - 1)]


def all_sum(value, axis, bits):
    size = lax.axis_size(axis)
    for bit in bits:
        value = value + lax.ppermute(value, axis, [(i, i ^ bit) for i in range(size)])
    return value


def is_one_of(index, wanted):
    hit = index == wanted[0]
    for other in wanted[1:]:
        hit = hit | (index == other)
    return hit


def choose(index, options):
    options = [o for o in options if o[1]]
    chosen = options[0][0]
    for value, wanted in options[1:]:
        chosen = jnp.where(is_one_of(index, wanted), value, chosen)
    return chosen


def step(logits, expression, spatial, density, slide_ids, spot_valid, neighbours):
    cells, spots = logits.shape
    genes = spatial.shape[0]
    gene_cols = expression.shape[1]
    n_spot, n_cell = lax.axis_size("spot"), lax.axis_size("cell")
    total_cells, total_spots = cells * n_cell, spots * n_spot
    lines, peers = n_spot, n_cell // n_spot
    few_peers = peers <= 2
    s = lax.axis_index("spot")
    k = lax.axis_index("cell")
    z, y = k // peers, k % peers
    offset = s * spots

    def turn(value, d):
        pairs = [(i, (i // peers) * peers + (i % peers + d) % peers) for i in range(n_cell)]
        return lax.ppermute(value, "cell", pairs)

    held = {0: expression}
    for bit in reversed(bits_of(n_spot)):
        pairs = [(i, i ^ bit) for i in range(n_spot)]
        held.update({m ^ bit: lax.ppermute(v, "spot", pairs) for m, v in list(held.items())})
    genes_all = jnp.concatenate(
        [choose(s, [(held[m], [i for i in range(n_spot) if i ^ m == j]) for m in held]) for j in range(n_spot)],
        axis=1,
    )
    (genes_all,) = apart(genes_all)

    def gene_block(block):
        return lax.dynamic_slice_in_dim(genes_all, block * genes, genes, axis=1)

    local_max = jnp.max(logits, axis=0)
    raised = jnp.exp(logits - local_max)
    local_sum = jnp.sum(raised, axis=0)
    (raised,) = apart(raised)
    own_pair = jnp.stack([local_max, local_sum])
    turned = [own_pair] + [turn(own_pair, d) for d in range(1, peers)]

    def joined(a, b):
        top = jnp.maximum(a[0], b[0])
        return jnp.stack([top, a[1] * jnp.exp(a[0] - top) + b[1] * jnp.exp(b[0] - top)])

    both = turned[0]
    for other in turned[1:]:
        both = joined(both, other)
    for bit in bits_of(lines):
        both = joined(both, lax.ppermute(both, "cell", [(i, i ^ (bit * peers)) for i in range(n_cell)]))
    scales = [jnp.exp(t[0] - both[0]) / both[1] for t in turned]
    mapping = raised * scales[0]

    frame = spots + 2 * SIDE
    valid_all = spot_valid.astype(jnp.float32)
    nvalid = jnp.sum(valid_all)
    reach = SIDE + ROW + 1
    wide_valid = lax.dynamic_slice_in_dim(jnp.pad(valid_all, reach), offset, spots + 2 * reach)
    wide_slide = lax.dynamic_slice_in_dim(
        jnp.pad(slide_ids, reach, constant_values=-1), offset, spots + 2 * reach
    )
    up_spot = [(i, i + 1) for i in range(n_spot - 1)]
    down_spot = [(i + 1, i) for i in range(n_spot - 1)]

    def framed(tile):
        before = lax.ppermute(tile[:, -SIDE:], "spot", up_spot)
        after = lax.ppermute(tile[:, :SIDE], "spot", down_spot)
        return jnp.concatenate([before, tile, after], axis=1)

    lists = framed(neighbours.T)
    spatial_wide = framed(spatial)
    spot_index = offset - SIDE + jnp.arange(frame, dtype=jnp.int32)
    inner = ROW + 1
    slide_frame = wide_slide[inner : inner + frame]
    valid_frame = wide_valid[inner : inner + frame]
    links = []
    for o in OFFSETS:
        listed = jnp.sum(((lists >= 0) & (lists == spot_index + o)).astype(jnp.float32), axis=0)
        there = wide_valid[inner + o : inner + o + frame] == 1.0
        same = wide_slide[inner + o : inner + o + frame] == slide_frame
        links.append(jnp.where(there & same, listed, 0.0))
    links = jnp.stack(links)
    counts = 1.0 + jnp.sum(links, axis=0)
    links, counts = apart(links, counts)
    valid_here = valid_frame[SIDE : SIDE + spots]
    slide_here = slide_frame[SIDE : SIDE + spots]
    members = (slide_here[None, :] == jnp.arange(SLIDES, dtype=jnp.int32)[:, None]).astype(jnp.float32)

    order = [sorted(range(lines), key=lambda t: (-abs(t - a), abs(2 * t - lines + 1))) for a in range(lines)]

    def part(block):
        return lax.dot_general(gene_block(block), raised, (((0,), (0,)), ((), ())), precision=highest)

    def line_pairs(pairs):
        return [(a * peers + c, b * peers + c) for a, b in pairs for c in range(peers)]

    def along(up_value, up_from, down_value, down_from):
        up_pairs = [(a, a + 1) for a in up_from]
        down_pairs = [(a, a - 1) for a in down_from]
        targets = {b for _, b in up_pairs} & {b for _, b in down_pairs}
        if targets or set(up_from) & set(down_from):
            return (
                lax.ppermute(up_value, "cell", line_pairs(up_pairs)),
                lax.ppermute(down_value, "cell", line_pairs(down_pairs)),
            )
        value = choose(z, [(up_value, list(up_from)), (down_value, list(down_from))])
        moved = lax.ppermute(value, "cell", line_pairs(up_pairs + down_pairs))
        return moved, moved

    if few_peers:
        units = []
        for u in range(lines):
            to = jnp.array([order[a][u] for a in range(lines)], jnp.int32)[z]
            sent = [turn(part(to * peers + (y + d) % peers), d) for d in range(1, peers)]
            unit = part(to * peers + y) * scales[0]
            for value, scale in zip(sent, scales[1:]):
                unit = unit + value * scale
            units.append(unit)

        def unit_for(target):
            wanted = [[] for _ in range(lines)]
            for a in range(lines):
                if 0 <= target(a) < lines:
                    wanted[order[a].index(target(a))].append(a)
            return choose(z, list(zip(units, wanted)))

        got_up = got_down = None
        for p in range(lines - 1, 0, -1):
            up_value, down_value = unit_for(lambda a: a + p), unit_for(lambda a: a - p)
            if got_up is not None:
                up_value, down_value = up_value + got_up, down_value + got_down
            got_up, got_down = along(up_value, range(0, lines - p), down_value, range(p, lines))
        predicted = unit_for(lambda a: a)
        if got_up is not None:
            predicted = predicted + got_up + got_down
    else:
        whole = lax.dot_general(genes_all, mapping, (((0,), (0,)), ((), ())), precision=highest)
        predicted = lax.psum_scatter(whole, "cell", scatter_dimension=0, tiled=True)

    wide = framed(predicted)

    def shifted(value, o):
        return jnp.pad(value, ((0, 0), (ROW + 1, ROW + 1)))[:, ROW + 1 + o : ROW + 1 + o + frame]

    summed = wide
    for i, o in enumerate(OFFSETS):
        summed = summed + links[i] * shifted(wide, o)
    smoothed_wide = summed / counts
    wide, smoothed_wide, spatial_wide = apart(wide, smoothed_wide, spatial_wide)
    spot_sums = jnp.stack(
        [
            jnp.sum(smoothed_wide * spatial_wide, axis=0),
            jnp.sum(smoothed_wide * smoothed_wide, axis=0),
            jnp.sum(spatial_wide * spatial_wide, axis=0),
            jnp.sum(wide, axis=0),
        ]
    )
    here = slice(SIDE, SIDE + spots)
    smoothed, weighted = smoothed_wide[:, here], valid_here[None, :]
    own_rows = spot_sums[3, here]
    gene_sums = jnp.concatenate(
        [
            jnp.sum(weighted * smoothed * spatial, axis=1),
            jnp.sum(weighted * smoothed * smoothed, axis=1),
            jnp.sum(weighted * spatial * spatial, axis=1),
            jnp.sum(members * (valid_here * own_rows)[None, :], axis=1),
            jnp.sum(members * (valid_here * density)[None, :], axis=1),
            jnp.sum(weighted * predicted * predicted)[None],
            jnp.sum(mapping * mapping * weighted)[None],
        ]
    )
    gene_sums = all_sum(gene_sums, "spot", bits_of(n_spot))
    spot_sums = all_sum(spot_sums, "cell", bits_of(n_cell))
    gene_inner, gene_own, gene_target = (gene_sums[i * genes : (i + 1) * genes] for i in range(3))
    row_part = gene_sums[3 * genes : 3 * genes + SLIDES]
    target_tot = gene_sums[3 * genes + SLIDES : 3 * genes + 2 * SLIDES]
    square_parts = gene_sums[3 * genes + 2 * SLIDES :]
    spot_inner, spot_own, spot_target, row_sums = (spot_sums[i] for i in range(4))
    row_sums = row_sums[here]
    gene_scale = lax.rsqrt((gene_own + epsilon) * (gene_target + epsilon))
    spot_scale = lax.rsqrt((spot_own + epsilon) * (spot_target + epsilon))
    cos_gene = gene_inner * gene_scale
    cos_spot = (spot_inner * spot_scale)[here]
    target = density / jnp.sum(members * target_tot[:, None], axis=0)
    by_gene = total_cells * gene_scale
    by_spot = total_cells * total_spots / nvalid * spot_scale
    spread_in = (
        -valid_frame
        / counts
        * (
            (spatial_wide - (gene_inner / (gene_own + epsilon))[:, None] * smoothed_wide) * by_gene[:, None]
            + (spatial_wide - (spot_inner / (spot_own + epsilon))[None, :] * smoothed_wide) * by_spot[None, :]
        )
    )
    (spread_in,) = apart(spread_in)
    spread = spread_in
    for i, o in enumerate(OFFSETS):
        spread = spread + shifted(links[i] * spread_in, -o)
    grad_pred = spread[:, here]
    (grad_pred,) = apart(grad_pred)

    kl_known = valid_here * target * (jnp.log(target) - jnp.log(row_sums))
    spot_part = jnp.concatenate(
        [
            jnp.sum(valid_here * cos_spot)[None],
            jnp.sum(kl_known)[None],
            jnp.sum(members * (valid_here * target)[None, :], axis=1),
        ]
    )
    spot_part = all_sum(spot_part, "spot", bits_of(n_spot))
    late = jnp.concatenate(
        [
            jnp.sum(predicted * grad_pred, axis=0),
            row_part,
            square_parts,
            jnp.sum(gene_own)[None],
            jnp.sum(cos_gene)[None],
        ]
    )
    late = all_sum(late, "cell", bits_of(n_cell))
    row_tot = late[spots : spots + SLIDES]
    slide_rows = jnp.sum(members * row_tot[:, None], axis=0)
    level = total_cells * total_spots * valid_here * (1.0 / slide_rows - target / row_sums)
    column_dot = late[:spots] + level * row_sums
    (mapping,) = apart(mapping)
    share = all_sum(jnp.sum(mapping * level[None, :], axis=1), "spot", bits_of(n_spot))

    grad_map = None
    if few_peers:
        far = [sorted((t for t in range(lines)), key=lambda t: (abs(t - a), t)) for a in range(lines)]
        ups, downs = [grad_pred], [grad_pred]
        for p in range(1, lines):
            up, down = along(ups[-1], range(p - 1, lines - 1), downs[-1], range(1, lines - p + 1))
            ups.append(up)
            downs.append(down)
        slots = []
        for u in range(lines):
            options = [(grad_pred, [])] + [(v, []) for v in ups[1:]] + [(v, []) for v in downs[1:]]
            for a in range(lines):
                t = far[a][u]
                at = 0 if t == a else (a - t if t < a else lines - 1 + t - a)
                options[at][1].append(a)
            slots.append(choose(z, options))
            slots[u], *passed = apart(slots[u], *ups[1 : u + 1], *downs[1 : u + 1])
            ups[1 : u + 1], downs[1 : u + 1] = passed[:u], passed[u:]

        kept = [None] * peers
        for u in range(lines):
            to = jnp.array([far[a][u] for a in range(lines)], jnp.int32)[z]
            blocks = [slots[u]] + [turn(slots[u], d) for d in range(1, peers)]
            for d, block in enumerate(blocks):
                names = to * peers + (y - d) % peers
                piece = jnp.dot(gene_block(names), block, precision=highest)
                grad_map = piece if grad_map is None else grad_map + piece
                wide_grad = lax.dot_general(mapping, block, (((1,), (1,)), ((), ())), precision=highest)
                for bit in bits_of(n_spot):
                    pairs = []
                    for i in range(n_cell):
                        t = far[i // peers][u]
                        for j in range(n_spot):
                            if (j ^ t) & (2 * bit - 1) == bit:
                                pairs.append((j * n_cell + i, (j ^ bit) * n_cell + i))
                    wide_grad = wide_grad + lax.ppermute(wide_grad, ("spot", "cell"), pairs)
                mine = s == to
                kept[d] = wide_grad if kept[d] is None else jnp.where(mine, wide_grad, kept[d])
        grad_expr = jnp.zeros((cells, gene_cols), jnp.float32)
        for d in range(peers):
            grad_expr = lax.dynamic_update_slice_in_dim(grad_expr, kept[d], ((y - d) % peers) * genes, axis=1)
    else:
        rows = lax.all_gather(grad_pred, "cell", axis=0, tiled=True)
        grad_map = jnp.dot(genes_all, rows, precision=highest)
        wide_grad = lax.dot_general(mapping, rows, (((1,), (1,)), ((), ())), precision=highest)
        grad_expr = lax.psum_scatter(wide_grad, "spot", scatter_dimension=1, tiled=True)
    gene_total = jnp.sum(genes_all, axis=1)
    grad_logits = mapping * (grad_map + (gene_total[:, None] * level[None, :] - column_dot[None, :]))
    grad_expr = grad_expr + share[:, None]

    pred_sq, map_sq, smooth_sq, cos_total = (late[spots + SLIDES + i] for i in range(4))
    gene_loss = 1.0 - cos_total / GENES
    spot_loss = 1.0 - spot_part[0] / nvalid
    density_loss = spot_part[1] + jnp.sum(jnp.where(row_tot > 0, spot_part[2:] * jnp.log(row_tot), 0.0))
    rms_weights = total_cells * jnp.sqrt(map_sq / (total_cells * nvalid))
    rms_pred = jnp.sqrt(pred_sq / (GENES * nvalid))
    rms_smooth = jnp.sqrt(smooth_sq / (GENES * nvalid))
    return (gene_loss, spot_loss, density_loss, grad_logits, grad_expr, rms_weights, rms_pred, rms_smooth)


def solution(mesh):
    placed = (
        P("cell", "spot"),
        P("cell", "spot"),
        P("cell", "spot"),
        P("spot"),
        P(),
        P(),
        P("spot", None),
    )
    step_map = jax.shard_map(
        step,
        mesh=mesh,
        in_specs=placed,
        out_specs=(P(), P(), P(), P("cell", "spot"), P("cell", "spot"), P(), P(), P()),
        check_vma=False,
    )
    if mesh.shape["cell"] > 2 * mesh.shape["spot"]:
        return step_map
    return step_map
```

```python
import jax
import jax.numpy as jnp
from jax import lax
from jax.sharding import PartitionSpec as P

GENES = 2048
ROW = 64
SLIDES = 3
SIDE = 2 * ROW
OFFSETS = (-ROW - 1, -ROW, -ROW + 1, -1, 1, ROW - 1, ROW, ROW + 1)

epsilon = 1e-06
highest = lax.Precision.HIGH


def apart(*values):
    return lax.optimization_barrier(values)


def bits_of(count):
    return [1 << b for b in range(count.bit_length() - 1)]


def all_sum(value, axis, bits):
    size = lax.axis_size(axis)
    for bit in bits:
        value = value + lax.ppermute(value, axis, [(i, i ^ bit) for i in range(size)])
    return value


def is_one_of(index, wanted):
    hit = index == wanted[0]
    for other in wanted[1:]:
        hit = hit | (index == other)
    return hit


def choose(index, options):
    options = [o for o in options if o[1]]
    chosen = options[0][0]
    for value, wanted in options[1:]:
        chosen = jnp.where(is_one_of(index, wanted), value, chosen)
    return chosen


def step(logits, expression, spatial, density, slide_ids, spot_valid, neighbours):
    cells, spots = logits.shape
    genes = spatial.shape[0]
    gene_cols = expression.shape[1]
    n_spot, n_cell = lax.axis_size("spot"), lax.axis_size("cell")
    total_cells, total_spots = cells * n_cell, spots * n_spot
    lines, peers = n_spot, n_cell // n_spot
    few_peers = peers <= 2
    s = lax.axis_index("spot")
    k = lax.axis_index("cell")
    z, y = k // peers, k % peers
    offset = s * spots

    def turn(value, d):
        pairs = [(i, (i // peers) * peers + (i % peers + d) % peers) for i in range(n_cell)]
        return lax.ppermute(value, "cell", pairs)

    order = [sorted(range(lines), key=lambda t: (-abs(t - a), abs(2 * t - lines + 1))) for a in range(lines)]
    far_line = jnp.array([order[a][0] for a in range(lines)], jnp.int32)[z]
    early = {}
    for d in range(1, peers if few_peers else 1):
        value = lax.dynamic_slice_in_dim(expression, ((y + d) % peers) * genes, genes, axis=1)
        left = n_spot - 1
        for bit in reversed(bits_of(n_spot)):
            pairs = [
                (j * n_cell + i, (j ^ bit) * n_cell + i)
                for i in range(n_cell)
                for j in range(n_spot)
                if (j ^ order[i // peers][0]) & left == 0
            ]
            got = lax.ppermute(value, ("spot", "cell"), pairs)
            value = jnp.where(((s ^ far_line) & left) == bit, got, value)
            left -= bit
        early[d] = value

    held = {0: expression}
    for bit in reversed(bits_of(n_spot)):
        pairs = [(i, i ^ bit) for i in range(n_spot)]
        held.update({m ^ bit: lax.ppermute(v, "spot", pairs) for m, v in list(held.items())})
    genes_all = jnp.concatenate(
        [choose(s, [(held[m], [i for i in range(n_spot) if i ^ m == j]) for m in held]) for j in range(n_spot)],
        axis=1,
    )
    (genes_all,) = apart(genes_all)

    def gene_block(block):
        return lax.dynamic_slice_in_dim(genes_all, block * genes, genes, axis=1)

    local_max = jnp.max(logits, axis=0)
    raised = jnp.exp(logits - local_max)
    local_sum = jnp.sum(raised, axis=0)
    (raised,) = apart(raised)
    own_pair = jnp.stack([local_max, local_sum])
    turned = [own_pair] + [turn(own_pair, d) for d in range(1, peers)]

    def joined(a, b):
        top = jnp.maximum(a[0], b[0])
        return jnp.stack([top, a[1] * jnp.exp(a[0] - top) + b[1] * jnp.exp(b[0] - top)])

    both = turned[0]
    for other in turned[1:]:
        both = joined(both, other)
    for bit in bits_of(lines):
        both = joined(both, lax.ppermute(both, "cell", [(i, i ^ (bit * peers)) for i in range(n_cell)]))
    scales = [jnp.exp(t[0] - both[0]) / both[1] for t in turned]
    mapping = raised * scales[0]

    frame = spots + 2 * SIDE
    valid_all = spot_valid.astype(jnp.float32)
    nvalid = jnp.sum(valid_all)
    reach = SIDE + ROW + 1
    wide_valid = lax.dynamic_slice_in_dim(jnp.pad(valid_all, reach), offset, spots + 2 * reach)
    wide_slide = lax.dynamic_slice_in_dim(
        jnp.pad(slide_ids, reach, constant_values=-1), offset, spots + 2 * reach
    )
    up_spot = [(i, i + 1) for i in range(n_spot - 1)]
    down_spot = [(i + 1, i) for i in range(n_spot - 1)]

    def framed(tile):
        before = lax.ppermute(tile[:, -SIDE:], "spot", up_spot)
        after = lax.ppermute(tile[:, :SIDE], "spot", down_spot)
        return jnp.concatenate([before, tile, after], axis=1)

    lists = framed(neighbours.T)
    spatial_wide = framed(spatial)
    spot_index = offset - SIDE + jnp.arange(frame, dtype=jnp.int32)
    inner = ROW + 1
    slide_frame = wide_slide[inner : inner + frame]
    valid_frame = wide_valid[inner : inner + frame]
    links = []
    for o in OFFSETS:
        listed = jnp.sum(((lists >= 0) & (lists == spot_index + o)).astype(jnp.float32), axis=0)
        there = wide_valid[inner + o : inner + o + frame] == 1.0
        same = wide_slide[inner + o : inner + o + frame] == slide_frame
        links.append(jnp.where(there & same, listed, 0.0))
    links = jnp.stack(links)
    counts = 1.0 + jnp.sum(links, axis=0)
    links, counts = apart(links, counts)
    valid_here = valid_frame[SIDE : SIDE + spots]
    slide_here = slide_frame[SIDE : SIDE + spots]
    members = (slide_here[None, :] == jnp.arange(SLIDES, dtype=jnp.int32)[:, None]).astype(jnp.float32)

    def part(block, columns=None):
        columns = gene_block(block) if columns is None else columns
        return lax.dot_general(columns, raised, (((0,), (0,)), ((), ())), precision=highest)

    def line_pairs(pairs):
        return [(a * peers + c, b * peers + c) for a, b in pairs for c in range(peers)]

    def along(up_value, up_from, down_value, down_from):
        up_pairs = [(a, a + 1) for a in up_from]
        down_pairs = [(a, a - 1) for a in down_from]
        targets = {b for _, b in up_pairs} & {b for _, b in down_pairs}
        if targets or set(up_from) & set(down_from):
            return (
                lax.ppermute(up_value, "cell", line_pairs(up_pairs)),
                lax.ppermute(down_value, "cell", line_pairs(down_pairs)),
            )
        value = choose(z, [(up_value, list(up_from)), (down_value, list(down_from))])
        moved = lax.ppermute(value, "cell", line_pairs(up_pairs + down_pairs))
        return moved, moved

    if few_peers:
        units = []
        for u in range(lines):
            to = jnp.array([order[a][u] for a in range(lines)], jnp.int32)[z]
            sent = [turn(part(to * peers + (y + d) % peers, None if u else early[d]), d) for d in range(1, peers)]
            unit = part(to * peers + y) * scales[0]
            for value, scale in zip(sent, scales[1:]):
                unit = unit + value * scale
            units.append(unit)

        def unit_for(target):
            wanted = [[] for _ in range(lines)]
            for a in range(lines):
                if 0 <= target(a) < lines:
                    wanted[order[a].index(target(a))].append(a)
            return choose(z, list(zip(units, wanted)))

        got_up = got_down = None
        for p in range(lines - 1, 0, -1):
            up_value, down_value = unit_for(lambda a: a + p), unit_for(lambda a: a - p)
            if got_up is not None:
                up_value, down_value = up_value + got_up, down_value + got_down
            got_up, got_down = along(up_value, range(0, lines - p), down_value, range(p, lines))
        predicted = unit_for(lambda a: a)
        if got_up is not None:
            predicted = predicted + got_up + got_down
    else:
        whole = lax.dot_general(genes_all, mapping, (((0,), (0,)), ((), ())), precision=highest)
        predicted = lax.psum_scatter(whole, "cell", scatter_dimension=0, tiled=True)

    wide = framed(predicted)

    def shifted(value, o):
        return jnp.pad(value, ((0, 0), (ROW + 1, ROW + 1)))[:, ROW + 1 + o : ROW + 1 + o + frame]

    summed = wide
    for i, o in enumerate(OFFSETS):
        summed = summed + links[i] * shifted(wide, o)
    smoothed_wide = summed / counts
    wide, smoothed_wide, spatial_wide = apart(wide, smoothed_wide, spatial_wide)
    spot_sums = jnp.stack(
        [
            jnp.sum(smoothed_wide * spatial_wide, axis=0),
            jnp.sum(smoothed_wide * smoothed_wide, axis=0),
            jnp.sum(spatial_wide * spatial_wide, axis=0),
            jnp.sum(wide, axis=0),
        ]
    )
    here = slice(SIDE, SIDE + spots)
    smoothed, weighted = smoothed_wide[:, here], valid_here[None, :]
    own_rows = spot_sums[3, here]
    gene_sums = jnp.concatenate(
        [
            jnp.sum(weighted * smoothed * spatial, axis=1),
            jnp.sum(weighted * smoothed * smoothed, axis=1),
            jnp.sum(weighted * spatial * spatial, axis=1),
            jnp.sum(members * (valid_here * own_rows)[None, :], axis=1),
            jnp.sum(members * (valid_here * density)[None, :], axis=1),
            jnp.sum(weighted * predicted * predicted)[None],
            jnp.sum(mapping * mapping * weighted)[None],
        ]
    )
    gene_sums = all_sum(gene_sums, "spot", bits_of(n_spot))
    spot_sums = all_sum(spot_sums, "cell", bits_of(n_cell))
    gene_inner, gene_own, gene_target = (gene_sums[i * genes : (i + 1) * genes] for i in range(3))
    row_part = gene_sums[3 * genes : 3 * genes + SLIDES]
    target_tot = gene_sums[3 * genes + SLIDES : 3 * genes + 2 * SLIDES]
    square_parts = gene_sums[3 * genes + 2 * SLIDES :]
    spot_inner, spot_own, spot_target, row_sums = (spot_sums[i] for i in range(4))
    row_sums = row_sums[here]
    gene_scale = lax.rsqrt((gene_own + epsilon) * (gene_target + epsilon))
    spot_scale = lax.rsqrt((spot_own + epsilon) * (spot_target + epsilon))
    cos_gene = gene_inner * gene_scale
    cos_spot = (spot_inner * spot_scale)[here]
    target = density / jnp.sum(members * target_tot[:, None], axis=0)
    by_gene = total_cells * gene_scale
    by_spot = total_cells * total_spots / nvalid * spot_scale
    spread_in = (
        -valid_frame
        / counts
        * (
            (spatial_wide - (gene_inner / (gene_own + epsilon))[:, None] * smoothed_wide) * by_gene[:, None]
            + (spatial_wide - (spot_inner / (spot_own + epsilon))[None, :] * smoothed_wide) * by_spot[None, :]
        )
    )
    (spread_in,) = apart(spread_in)
    spread = spread_in
    for i, o in enumerate(OFFSETS):
        spread = spread + shifted(links[i] * spread_in, -o)
    grad_pred = spread[:, here]
    (grad_pred,) = apart(grad_pred)

    kl_known = valid_here * target * (jnp.log(target) - jnp.log(row_sums))
    spot_part = jnp.concatenate(
        [
            jnp.sum(valid_here * cos_spot)[None],
            jnp.sum(kl_known)[None],
            jnp.sum(members * (valid_here * target)[None, :], axis=1),
        ]
    )
    spot_part = all_sum(spot_part, "spot", bits_of(n_spot))
    late = jnp.concatenate(
        [
            jnp.sum(predicted * grad_pred, axis=0),
            row_part,
            square_parts,
            jnp.sum(gene_own)[None],
            jnp.sum(cos_gene)[None],
        ]
    )
    late = all_sum(late, "cell", bits_of(n_cell))
    row_tot = late[spots : spots + SLIDES]
    slide_rows = jnp.sum(members * row_tot[:, None], axis=0)
    level = total_cells * total_spots * valid_here * (1.0 / slide_rows - target / row_sums)
    column_dot = late[:spots] + level * row_sums
    (mapping,) = apart(mapping)
    share = all_sum(jnp.sum(mapping * level[None, :], axis=1), "spot", bits_of(n_spot))

    grad_map = None
    if few_peers:
        far = [sorted((t for t in range(lines)), key=lambda t: (abs(t - a), t)) for a in range(lines)]
        ups, downs = [grad_pred], [grad_pred]
        for p in range(1, lines):
            up, down = along(ups[-1], range(p - 1, lines - 1), downs[-1], range(1, lines - p + 1))
            ups.append(up)
            downs.append(down)
        slots = []
        for u in range(lines):
            options = [(grad_pred, [])] + [(v, []) for v in ups[1:]] + [(v, []) for v in downs[1:]]
            for a in range(lines):
                t = far[a][u]
                at = 0 if t == a else (a - t if t < a else lines - 1 + t - a)
                options[at][1].append(a)
            slots.append(choose(z, options))
            slots[u], *passed = apart(slots[u], *ups[1 : u + 1], *downs[1 : u + 1])
            ups[1 : u + 1], downs[1 : u + 1] = passed[:u], passed[u:]

        kept = [None] * peers
        for u in range(lines):
            to = jnp.array([far[a][u] for a in range(lines)], jnp.int32)[z]
            blocks = [slots[u]] + [turn(slots[u], d) for d in range(1, peers)]
            for d, block in enumerate(blocks):
                names = to * peers + (y - d) % peers
                piece = jnp.dot(gene_block(names), block, precision=highest)
                grad_map = piece if grad_map is None else grad_map + piece
                wide_grad = lax.dot_general(mapping, block, (((1,), (1,)), ((), ())), precision=highest)
                for bit in bits_of(n_spot):
                    pairs = []
                    for i in range(n_cell):
                        t = far[i // peers][u]
                        for j in range(n_spot):
                            if (j ^ t) & (2 * bit - 1) == bit:
                                pairs.append((j * n_cell + i, (j ^ bit) * n_cell + i))
                    wide_grad = wide_grad + lax.ppermute(wide_grad, ("spot", "cell"), pairs)
                mine = s == to
                kept[d] = wide_grad if kept[d] is None else jnp.where(mine, wide_grad, kept[d])
        grad_expr = jnp.zeros((cells, gene_cols), jnp.float32)
        for d in range(peers):
            grad_expr = lax.dynamic_update_slice_in_dim(grad_expr, kept[d], ((y - d) % peers) * genes, axis=1)
    else:
        rows = lax.all_gather(grad_pred, "cell", axis=0, tiled=True)
        grad_map = jnp.dot(genes_all, rows, precision=highest)
        wide_grad = lax.dot_general(mapping, rows, (((1,), (1,)), ((), ())), precision=highest)
        grad_expr = lax.psum_scatter(wide_grad, "spot", scatter_dimension=1, tiled=True)
    gene_total = jnp.sum(genes_all, axis=1)
    grad_logits = mapping * (grad_map + (gene_total[:, None] * level[None, :] - column_dot[None, :]))
    grad_expr = grad_expr + share[:, None]

    pred_sq, map_sq, smooth_sq, cos_total = (late[spots + SLIDES + i] for i in range(4))
    gene_loss = 1.0 - cos_total / GENES
    spot_loss = 1.0 - spot_part[0] / nvalid
    density_loss = spot_part[1] + jnp.sum(jnp.where(row_tot > 0, spot_part[2:] * jnp.log(row_tot), 0.0))
    rms_weights = total_cells * jnp.sqrt(map_sq / (total_cells * nvalid))
    rms_pred = jnp.sqrt(pred_sq / (GENES * nvalid))
    rms_smooth = jnp.sqrt(smooth_sq / (GENES * nvalid))
    return (gene_loss, spot_loss, density_loss, grad_logits, grad_expr, rms_weights, rms_pred, rms_smooth)


def solution(mesh):
    placed = (
        P("cell", "spot"),
        P("cell", "spot"),
        P("cell", "spot"),
        P("spot"),
        P(),
        P(),
        P("spot", None),
    )
    step_map = jax.shard_map(
        step,
        mesh=mesh,
        in_specs=placed,
        out_specs=(P(), P(), P(), P("cell", "spot"), P("cell", "spot"), P(), P(), P()),
        check_vma=False,
    )
    if mesh.shape["cell"] > 2 * mesh.shape["spot"]:
        return step_map
    return step_map
```

```python
import jax
import jax.numpy as jnp
from jax import lax
from jax.experimental import pallas as pl
from jax.experimental.pallas import tpu as pltpu
from jax.sharding import PartitionSpec as P

GENES = 2048
ROW = 64
SLIDES = 3
SIDE = 2 * ROW
OFFSETS = (-ROW - 1, -ROW, -ROW + 1, -1, 1, ROW - 1, ROW, ROW + 1)

epsilon = 1e-06
highest = lax.Precision.HIGHEST


def apart(*values):
    return lax.optimization_barrier(values)


def bits_of(count):
    return [1 << b for b in range(count.bit_length() - 1)]


def all_sum(value, axis, bits):
    size = lax.axis_size(axis)
    for bit in bits:
        value = value + lax.ppermute(value, axis, [(i, i ^ bit) for i in range(size)])
    return value


def is_one_of(index, wanted):
    hit = index == wanted[0]
    for other in wanted[1:]:
        hit = hit | (index == other)
    return hit


def choose(index, options):
    options = [o for o in options if o[1]]
    chosen = options[0][0]
    for value, wanted in options[1:]:
        chosen = jnp.where(is_one_of(index, wanted), value, chosen)
    return chosen


def smooth_kernel(links, rows, before, tile, after, spatial, smoothed, spot_sums, gene_sums):
    frame = spatial.shape[1]
    value = jnp.concatenate([before[...], tile[...], after[...]], axis=1)
    total = value
    for i, o in enumerate(OFFSETS):
        total = total + links[i : i + 1, :] * pltpu.roll(value, (-o) % frame, 1)
    smooth = total / rows[0:1, :]
    smoothed[...] = smooth
    there = spatial[...]
    inner, own = smooth * there, smooth * smooth

    @pl.when(pl.program_id(0) == 0)
    def _():
        spot_sums[...] = jnp.zeros_like(spot_sums)

    for i, part in enumerate((inner, own, there * there, value)):
        spot_sums[i : i + 1, :] += jnp.sum(part, axis=0, keepdims=True)
    here = slice(SIDE, frame - SIDE)
    valid = rows[1:2, here]
    lane = lax.broadcasted_iota(jnp.int32, gene_sums.shape, 1)
    sums = jnp.zeros(gene_sums.shape, jnp.float32)
    for i, part in enumerate((inner, own, there * there, value * value)):
        sums = jnp.where(lane == i, jnp.sum(valid * part[:, here], axis=1, keepdims=True), sums)
    gene_sums[...] = sums


def smooth_call(links, rows, before, tile, after, spatial):
    genes, frame = spatial.shape
    step = min(32, genes)
    whole = lambda a: pl.BlockSpec(a.shape, lambda i: (0, 0))
    some = lambda width: pl.BlockSpec((step, width), lambda i: (i, 0))
    return pl.pallas_call(
        smooth_kernel,
        grid=(genes // step,),
        in_specs=[whole(links), whole(rows), some(SIDE), some(tile.shape[1]), some(SIDE), some(frame)],
        out_specs=[some(frame), pl.BlockSpec((4, frame), lambda i: (0, 0)), some(128)],
        out_shape=[
            jax.ShapeDtypeStruct((genes, frame), jnp.float32),
            jax.ShapeDtypeStruct((4, frame), jnp.float32),
            jax.ShapeDtypeStruct((genes, 128), jnp.float32),
        ],
        name="smooth",
    )(links, rows, before, tile, after, spatial)


def spread_kernel(links, rows, gene_rows, smoothed, spatial, tile, gradient, dots):
    frame = spatial.shape[1]
    smooth, there = smoothed[...], spatial[...]
    spread_in = rows[0:1, :] * (
        (there - gene_rows[:, 1:2] * smooth) * gene_rows[:, 0:1] + (there - rows[2:3, :] * smooth) * rows[1:2, :]
    )
    spread = spread_in
    for i, o in enumerate(OFFSETS):
        spread = spread + pltpu.roll(links[i : i + 1, :] * spread_in, o % frame, 1)
    spread = spread[:, SIDE : frame - SIDE]
    gradient[...] = spread

    @pl.when(pl.program_id(0) == 0)
    def _():
        dots[...] = jnp.zeros_like(dots)

    dots[...] += jnp.sum(spread * tile[...], axis=0, keepdims=True)


def spread_call(links, rows, gene_rows, smoothed, spatial, tile):
    genes, frame = spatial.shape
    step, spots = min(32, genes), tile.shape[1]
    whole = lambda a: pl.BlockSpec(a.shape, lambda i: (0, 0))
    some = lambda width: pl.BlockSpec((step, width), lambda i: (i, 0))
    return pl.pallas_call(
        spread_kernel,
        grid=(genes // step,),
        in_specs=[whole(links), whole(rows), some(2), some(frame), some(frame), some(spots)],
        out_specs=[some(spots), pl.BlockSpec((1, spots), lambda i: (0, 0))],
        out_shape=[
            jax.ShapeDtypeStruct((genes, spots), jnp.float32),
            jax.ShapeDtypeStruct((1, spots), jnp.float32),
        ],
        name="spread",
    )(links, rows, gene_rows, smoothed, spatial, tile)


def step(logits, expression, spatial, density, slide_ids, spot_valid, neighbours):
    cells, spots = logits.shape
    genes = spatial.shape[0]
    gene_cols = expression.shape[1]
    n_spot, n_cell = lax.axis_size("spot"), lax.axis_size("cell")
    total_cells, total_spots = cells * n_cell, spots * n_spot
    lines, peers = n_spot, n_cell // n_spot
    few_peers = peers <= 2
    s = lax.axis_index("spot")
    k = lax.axis_index("cell")
    z, y = k // peers, k % peers
    offset = s * spots

    def turn(value, d):
        pairs = [(i, (i // peers) * peers + (i % peers + d) % peers) for i in range(n_cell)]
        return lax.ppermute(value, "cell", pairs)

    order = [sorted(range(lines), key=lambda t: (-abs(t - a), abs(2 * t - lines + 1))) for a in range(lines)]
    far_line = jnp.array([order[a][0] for a in range(lines)], jnp.int32)[z]
    early = {}
    for d in range(1, peers if few_peers else 1):
        value = lax.dynamic_slice_in_dim(expression, ((y + d) % peers) * genes, genes, axis=1)
        left = n_spot - 1
        for bit in reversed(bits_of(n_spot)):
            pairs = [
                (j * n_cell + i, (j ^ bit) * n_cell + i)
                for i in range(n_cell)
                for j in range(n_spot)
                if (j ^ order[i // peers][0]) & left == 0
            ]
            got = lax.ppermute(value, ("spot", "cell"), pairs)
            value = jnp.where(((s ^ far_line) & left) == bit, got, value)
            left -= bit
        early[d] = value

    held = {0: expression}
    for bit in reversed(bits_of(n_spot)):
        pairs = [(i, i ^ bit) for i in range(n_spot)]
        held.update({m ^ bit: lax.ppermute(v, "spot", pairs) for m, v in list(held.items())})
    genes_all = jnp.concatenate(
        [choose(s, [(held[m], [i for i in range(n_spot) if i ^ m == j]) for m in held]) for j in range(n_spot)],
        axis=1,
    )
    (genes_all,) = apart(genes_all)

    def gene_block(block):
        return lax.dynamic_slice_in_dim(genes_all, block * genes, genes, axis=1)

    local_max = jnp.max(logits, axis=0)
    raised = jnp.exp(logits - local_max)
    local_sum = jnp.sum(raised, axis=0)
    (raised,) = apart(raised)
    own_pair = jnp.stack([local_max, local_sum])
    turned = [own_pair] + [turn(own_pair, d) for d in range(1, peers)]

    def joined(a, b):
        top = jnp.maximum(a[0], b[0])
        return jnp.stack([top, a[1] * jnp.exp(a[0] - top) + b[1] * jnp.exp(b[0] - top)])

    both = turned[0]
    for other in turned[1:]:
        both = joined(both, other)
    for bit in bits_of(lines):
        both = joined(both, lax.ppermute(both, "cell", [(i, i ^ (bit * peers)) for i in range(n_cell)]))
    scales = [jnp.exp(t[0] - both[0]) / both[1] for t in turned]
    mapping = raised * scales[0]

    frame = spots + 2 * SIDE
    valid_all = spot_valid.astype(jnp.float32)
    nvalid = jnp.sum(valid_all)
    reach = SIDE + ROW + 1
    wide_valid = lax.dynamic_slice_in_dim(jnp.pad(valid_all, reach), offset, spots + 2 * reach)
    wide_slide = lax.dynamic_slice_in_dim(
        jnp.pad(slide_ids, reach, constant_values=-1), offset, spots + 2 * reach
    )
    up_spot = [(i, i + 1) for i in range(n_spot - 1)]
    down_spot = [(i + 1, i) for i in range(n_spot - 1)]

    def sides(tile):
        before = lax.ppermute(tile[:, -SIDE:], "spot", up_spot)
        after = lax.ppermute(tile[:, :SIDE], "spot", down_spot)
        return before, tile, after

    def framed(tile):
        return jnp.concatenate(sides(tile), axis=1)

    lists = framed(neighbours.T)
    spatial_wide = framed(spatial)
    spot_index = offset - SIDE + jnp.arange(frame, dtype=jnp.int32)
    inner = ROW + 1
    slide_frame = wide_slide[inner : inner + frame]
    valid_frame = wide_valid[inner : inner + frame]
    links = []
    for o in OFFSETS:
        listed = jnp.sum(((lists >= 0) & (lists == spot_index + o)).astype(jnp.float32), axis=0)
        there = wide_valid[inner + o : inner + o + frame] == 1.0
        same = wide_slide[inner + o : inner + o + frame] == slide_frame
        links.append(jnp.where(there & same, listed, 0.0))
    links = jnp.stack(links)
    counts = 1.0 + jnp.sum(links, axis=0)
    links, counts = apart(links, counts)
    valid_here = valid_frame[SIDE : SIDE + spots]
    slide_here = slide_frame[SIDE : SIDE + spots]
    members = (slide_here[None, :] == jnp.arange(SLIDES, dtype=jnp.int32)[:, None]).astype(jnp.float32)
    here, weighted = slice(SIDE, SIDE + spots), valid_here[None, :]
    early_sums = jnp.concatenate(
        [
            jnp.sum(members * (valid_here * density)[None, :], axis=1),
            jnp.sum(mapping * mapping * weighted)[None],
        ]
    )
    early_sums = all_sum(early_sums, "spot", bits_of(n_spot))
    target = density / jnp.sum(members * early_sums[:SLIDES, None], axis=0)
    frame_rows = jnp.stack([counts, valid_frame])
    links, frame_rows, spatial_wide, target = apart(links, frame_rows, spatial_wide, target)

    def part(block, columns=None):
        columns = gene_block(block) if columns is None else columns
        return lax.dot_general(columns, raised, (((0,), (0,)), ((), ())), precision=highest)

    def line_pairs(pairs):
        return [(a * peers + c, b * peers + c) for a, b in pairs for c in range(peers)]

    def along(up_value, up_from, down_value, down_from):
        up_pairs = [(a, a + 1) for a in up_from]
        down_pairs = [(a, a - 1) for a in down_from]
        targets = {b for _, b in up_pairs} & {b for _, b in down_pairs}
        if targets or set(up_from) & set(down_from):
            return (
                lax.ppermute(up_value, "cell", line_pairs(up_pairs)),
                lax.ppermute(down_value, "cell", line_pairs(down_pairs)),
            )
        value = choose(z, [(up_value, list(up_from)), (down_value, list(down_from))])
        moved = lax.ppermute(value, "cell", line_pairs(up_pairs + down_pairs))
        return moved, moved

    if few_peers:
        units = []
        for u in range(lines):
            to = jnp.array([order[a][u] for a in range(lines)], jnp.int32)[z]
            sent = [turn(part(to * peers + (y + d) % peers, None if u else early[d]), d) for d in range(1, peers)]
            unit = part(to * peers + y) * scales[0]
            for value, scale in zip(sent, scales[1:]):
                unit = unit + value * scale
            units.append(unit)

        def unit_for(target):
            wanted = [[] for _ in range(lines)]
            for a in range(lines):
                if 0 <= target(a) < lines:
                    wanted[order[a].index(target(a))].append(a)
            return choose(z, list(zip(units, wanted)))

        got_up = got_down = None
        for p in range(lines - 1, 0, -1):
            up_value, down_value = unit_for(lambda a: a + p), unit_for(lambda a: a - p)
            if got_up is not None:
                up_value, down_value = up_value + got_up, down_value + got_down
            got_up, got_down = along(up_value, range(0, lines - p), down_value, range(p, lines))
        predicted = unit_for(lambda a: a)
        if got_up is not None:
            predicted = predicted + got_up + got_down
    else:
        whole = lax.dot_general(genes_all, mapping, (((0,), (0,)), ((), ())), precision=highest)
        predicted = lax.psum_scatter(whole, "cell", scatter_dimension=0, tiled=True)

    smoothed_wide, spot_sums, gene_sums = smooth_call(links, frame_rows, *sides(predicted), spatial_wide)
    gene_sums = all_sum(gene_sums[:, :4].T, "spot", bits_of(n_spot))
    spot_sums = all_sum(spot_sums, "cell", bits_of(n_cell))
    gene_inner, gene_own, gene_target, pred_squares = (gene_sums[i] for i in range(4))
    spot_inner, spot_own, spot_target, row_sums = (spot_sums[i] for i in range(4))
    row_sums = row_sums[here]
    gene_scale = lax.rsqrt((gene_own + epsilon) * (gene_target + epsilon))
    spot_scale = lax.rsqrt((spot_own + epsilon) * (spot_target + epsilon))
    cos_gene = gene_inner * gene_scale
    cos_spot = (spot_inner * spot_scale)[here]
    by_gene = total_cells * gene_scale
    by_spot = total_cells * total_spots / nvalid * spot_scale
    frame_rows = jnp.stack([-valid_frame / counts, by_spot, spot_inner / (spot_own + epsilon)])
    gene_rows = jnp.stack([by_gene, gene_inner / (gene_own + epsilon)], axis=1)
    grad_pred, dots = spread_call(links, frame_rows, gene_rows, smoothed_wide, spatial_wide, predicted)

    kl_known = valid_here * target * (jnp.log(target) - jnp.log(row_sums))
    spot_part = jnp.concatenate(
        [
            jnp.sum(valid_here * cos_spot)[None],
            jnp.sum(kl_known)[None],
            jnp.sum(members * (valid_here * target)[None, :], axis=1),
            jnp.sum(members * (valid_here * row_sums)[None, :], axis=1),
        ]
    )
    spot_part = all_sum(spot_part, "spot", bits_of(n_spot))
    late = jnp.concatenate(
        [
            dots[0],
            jnp.sum(pred_squares)[None],
            early_sums[SLIDES:],
            jnp.sum(gene_own)[None],
            jnp.sum(cos_gene)[None],
        ]
    )
    late = all_sum(late, "cell", bits_of(n_cell))
    row_tot = spot_part[2 + SLIDES :]
    slide_rows = jnp.sum(members * row_tot[:, None], axis=0)
    level = total_cells * total_spots * valid_here * (1.0 / slide_rows - target / row_sums)
    column_dot = late[:spots] + level * row_sums
    (mapping,) = apart(mapping)
    share = all_sum(jnp.sum(mapping * level[None, :], axis=1), "spot", bits_of(n_spot))

    grad_map = None
    if few_peers:
        far = [sorted((t for t in range(lines)), key=lambda t: (abs(t - a), t)) for a in range(lines)]
        ups, downs = [grad_pred], [grad_pred]
        for p in range(1, lines):
            up, down = along(ups[-1], range(p - 1, lines - 1), downs[-1], range(1, lines - p + 1))
            ups.append(up)
            downs.append(down)
        slots = []
        for u in range(lines):
            options = [(grad_pred, [])] + [(v, []) for v in ups[1:]] + [(v, []) for v in downs[1:]]
            for a in range(lines):
                t = far[a][u]
                at = 0 if t == a else (a - t if t < a else lines - 1 + t - a)
                options[at][1].append(a)
            slots.append(choose(z, options))
            slots[u], *passed = apart(slots[u], *ups[1 : u + 1], *downs[1 : u + 1])
            ups[1 : u + 1], downs[1 : u + 1] = passed[:u], passed[u:]

        kept = [None] * peers
        for u in range(lines):
            to = jnp.array([far[a][u] for a in range(lines)], jnp.int32)[z]
            blocks = [slots[u]] + [turn(slots[u], d) for d in range(1, peers)]
            for d, block in enumerate(blocks):
                names = to * peers + (y - d) % peers
                piece = jnp.dot(gene_block(names), block, precision=highest)
                grad_map = piece if grad_map is None else grad_map + piece
                wide_grad = lax.dot_general(mapping, block, (((1,), (1,)), ((), ())), precision=highest)
                for bit in bits_of(n_spot):
                    pairs = []
                    for i in range(n_cell):
                        t = far[i // peers][u]
                        for j in range(n_spot):
                            if (j ^ t) & (2 * bit - 1) == bit:
                                pairs.append((j * n_cell + i, (j ^ bit) * n_cell + i))
                    wide_grad = wide_grad + lax.ppermute(wide_grad, ("spot", "cell"), pairs)
                mine = s == to
                kept[d] = wide_grad if kept[d] is None else jnp.where(mine, wide_grad, kept[d])
        grad_expr = jnp.zeros((cells, gene_cols), jnp.float32)
        for d in range(peers):
            grad_expr = lax.dynamic_update_slice_in_dim(grad_expr, kept[d], ((y - d) % peers) * genes, axis=1)
    else:
        rows = lax.all_gather(grad_pred, "cell", axis=0, tiled=True)
        grad_map = jnp.dot(genes_all, rows, precision=highest)
        wide_grad = lax.dot_general(mapping, rows, (((1,), (1,)), ((), ())), precision=highest)
        grad_expr = lax.psum_scatter(wide_grad, "spot", scatter_dimension=1, tiled=True)
    gene_total = jnp.sum(genes_all, axis=1)
    grad_logits = mapping * (grad_map + (gene_total[:, None] * level[None, :] - column_dot[None, :]))
    grad_expr = grad_expr + share[:, None]

    pred_sq, map_sq, smooth_sq, cos_total = (late[spots + i] for i in range(4))
    gene_loss = 1.0 - cos_total / GENES
    spot_loss = 1.0 - spot_part[0] / nvalid
    density_loss = spot_part[1] + jnp.sum(jnp.where(row_tot > 0, spot_part[2 : 2 + SLIDES] * jnp.log(row_tot), 0.0))
    rms_weights = total_cells * jnp.sqrt(map_sq / (total_cells * nvalid))
    rms_pred = jnp.sqrt(pred_sq / (GENES * nvalid))
    rms_smooth = jnp.sqrt(smooth_sq / (GENES * nvalid))
    return (gene_loss, spot_loss, density_loss, grad_logits, grad_expr, rms_weights, rms_pred, rms_smooth)


def solution(mesh):
    placed = (
        P("cell", "spot"),
        P("cell", "spot"),
        P("cell", "spot"),
        P("spot"),
        P(),
        P(),
        P("spot", None),
    )
    step_map = jax.shard_map(
        step,
        mesh=mesh,
        in_specs=placed,
        out_specs=(P(), P(), P(), P("cell", "spot"), P("cell", "spot"), P(), P(), P()),
        check_vma=False,
    )
    if mesh.shape["cell"] > 2 * mesh.shape["spot"]:
        return step_map
    return step_map
```

```python
import jax
import jax.numpy as jnp
from jax import lax
from jax.experimental import pallas as pl
from jax.experimental.pallas import tpu as pltpu
from jax.sharding import PartitionSpec as P

GENES = 2048
ROW = 64
SLIDES = 3
SIDE = 2 * ROW
OFFSETS = (-ROW - 1, -ROW, -ROW + 1, -1, 1, ROW - 1, ROW, ROW + 1)

epsilon = 1e-06
highest = lax.Precision.HIGHEST


def apart(*values):
    return lax.optimization_barrier(values)


def bits_of(count):
    return [1 << b for b in range(count.bit_length() - 1)]


def all_sum(value, axis, bits):
    size = lax.axis_size(axis)
    for bit in bits:
        value = value + lax.ppermute(value, axis, [(i, i ^ bit) for i in range(size)])
    return value


def is_one_of(index, wanted):
    hit = index == wanted[0]
    for other in wanted[1:]:
        hit = hit | (index == other)
    return hit


def entry(index, values):
    picked = jnp.int32(values[0])
    for i, value in enumerate(values[1:], 1):
        picked = jnp.where(index == i, jnp.int32(value), picked)
    return picked


def choose(index, options):
    options = [o for o in options if o[1]]
    chosen = options[0][0]
    for value, wanted in options[1:]:
        chosen = jnp.where(is_one_of(index, wanted), value, chosen)
    return chosen


def smooth_kernel(links, rows, before, tile, after, spatial, smoothed, spot_sums, gene_sums, parts):
    frame = spatial.shape[1]
    here = slice(SIDE, frame - SIDE)
    lane = lax.broadcasted_iota(jnp.int32, (8, 128), 1)

    @pl.when(pl.program_id(0) == 0)
    def _():
        parts[...] = jnp.zeros_like(parts)

    def group(g, carry):
        at = pl.ds(pl.multiple_of(g * 8, 8), 8)
        value = jnp.concatenate([before[at, :], tile[at, :], after[at, :]], axis=1)
        total = value
        for i, o in enumerate(OFFSETS):
            total = total + links[i : i + 1, :] * pltpu.roll(value, (-o) % frame, 1)
        smooth = total / rows[0:1, :]
        smoothed[at, :] = smooth
        there = spatial[at, :]
        inner, own, target = smooth * there, smooth * smooth, there * there
        for i, part in enumerate((inner, own, target, value)):
            parts[8 * i : 8 * i + 8, :] += part
        valid = rows[1:2, here]
        sums = jnp.zeros((8, 128), jnp.float32)
        for i, part in enumerate((inner, own, target, value * value)):
            sums = jnp.where(lane == i, jnp.sum(valid * part[:, here], axis=1, keepdims=True), sums)
        gene_sums[at, :] = sums
        return carry

    lax.fori_loop(0, tile.shape[0] // 8, group, 0)

    @pl.when(pl.program_id(0) == pl.num_programs(0) - 1)
    def _():
        for i in range(4):
            spot_sums[i : i + 1, :] = jnp.sum(parts[8 * i : 8 * i + 8, :], axis=0, keepdims=True)


def smooth_call(links, rows, before, tile, after, spatial):
    genes, frame = spatial.shape
    step = min(64, genes)
    whole = lambda a: pl.BlockSpec(a.shape, lambda i: (0, 0))
    some = lambda width: pl.BlockSpec((step, width), lambda i: (i, 0))
    return pl.pallas_call(
        smooth_kernel,
        grid=(genes // step,),
        in_specs=[whole(links), whole(rows), some(SIDE), some(tile.shape[1]), some(SIDE), some(frame)],
        out_specs=[some(frame), pl.BlockSpec((4, frame), lambda i: (0, 0)), some(128)],
        out_shape=[
            jax.ShapeDtypeStruct((genes, frame), jnp.float32),
            jax.ShapeDtypeStruct((4, frame), jnp.float32),
            jax.ShapeDtypeStruct((genes, 128), jnp.float32),
        ],
        scratch_shapes=[pltpu.VMEM((32, frame), jnp.float32)],
        name="smooth",
    )(links, rows, before, tile, after, spatial)


def spread_kernel(links, rows, gene_rows, smoothed, spatial, tile, gradient, dots, parts):
    frame = spatial.shape[1]

    @pl.when(pl.program_id(0) == 0)
    def _():
        parts[...] = jnp.zeros_like(parts)

    def group(g, carry):
        at = pl.ds(pl.multiple_of(g * 8, 8), 8)
        smooth, there = smoothed[at, :], spatial[at, :]
        spread_in = rows[0:1, :] * (
            (there - gene_rows[at, 1:2] * smooth) * gene_rows[at, 0:1] + (there - rows[2:3, :] * smooth) * rows[1:2, :]
        )
        spread = spread_in
        for i, o in enumerate(OFFSETS):
            spread = spread + pltpu.roll(links[i : i + 1, :] * spread_in, o % frame, 1)
        spread = spread[:, SIDE : frame - SIDE]
        gradient[at, :] = spread
        parts[...] += spread * tile[at, :]
        return carry

    lax.fori_loop(0, tile.shape[0] // 8, group, 0)

    @pl.when(pl.program_id(0) == pl.num_programs(0) - 1)
    def _():
        dots[...] = jnp.sum(parts[...], axis=0, keepdims=True)


def spread_call(links, rows, gene_rows, smoothed, spatial, tile):
    genes, frame = spatial.shape
    step, spots = min(64, genes), tile.shape[1]
    whole = lambda a: pl.BlockSpec(a.shape, lambda i: (0, 0))
    some = lambda width: pl.BlockSpec((step, width), lambda i: (i, 0))
    return pl.pallas_call(
        spread_kernel,
        grid=(genes // step,),
        in_specs=[whole(links), whole(rows), some(2), some(frame), some(frame), some(spots)],
        out_specs=[some(spots), pl.BlockSpec((1, spots), lambda i: (0, 0))],
        out_shape=[
            jax.ShapeDtypeStruct((genes, spots), jnp.float32),
            jax.ShapeDtypeStruct((1, spots), jnp.float32),
        ],
        scratch_shapes=[pltpu.VMEM((8, spots), jnp.float32)],
        name="spread",
    )(links, rows, gene_rows, smoothed, spatial, tile)


def step(logits, expression, spatial, density, slide_ids, spot_valid, neighbours):
    cells, spots = logits.shape
    genes = spatial.shape[0]
    gene_cols = expression.shape[1]
    n_spot, n_cell = lax.axis_size("spot"), lax.axis_size("cell")
    total_cells, total_spots = cells * n_cell, spots * n_spot
    lines, peers = n_spot, n_cell // n_spot
    few_peers = peers <= 2
    s = lax.axis_index("spot")
    k = lax.axis_index("cell")
    z, y = k // peers, k % peers
    offset = s * spots

    def turn(value, d):
        pairs = [(i, (i // peers) * peers + (i % peers + d) % peers) for i in range(n_cell)]
        return lax.ppermute(value, "cell", pairs)

    order = [sorted(range(lines), key=lambda t: (-abs(t - a), abs(2 * t - lines + 1))) for a in range(lines)]
    far_line = entry(z, [order[a][0] for a in range(lines)])
    early = {}
    for d in range(1, peers if few_peers else 1):
        value = lax.dynamic_slice_in_dim(expression, ((y + d) % peers) * genes, genes, axis=1)
        left = n_spot - 1
        for bit in reversed(bits_of(n_spot)):
            pairs = [
                (j * n_cell + i, (j ^ bit) * n_cell + i)
                for i in range(n_cell)
                for j in range(n_spot)
                if (j ^ order[i // peers][0]) & left == 0
            ]
            got = lax.ppermute(value, ("spot", "cell"), pairs)
            value = jnp.where(((s ^ far_line) & left) == bit, got, value)
            left -= bit
        early[d] = value

    held = {0: expression}
    for bit in reversed(bits_of(n_spot)):
        pairs = [(i, i ^ bit) for i in range(n_spot)]
        held.update({m ^ bit: lax.ppermute(v, "spot", pairs) for m, v in list(held.items())})
    genes_all = jnp.concatenate(
        [choose(s, [(held[m], [i for i in range(n_spot) if i ^ m == j]) for m in held]) for j in range(n_spot)],
        axis=1,
    )
    (genes_all,) = apart(genes_all)

    def gene_block(block):
        return lax.dynamic_slice_in_dim(genes_all, block * genes, genes, axis=1)

    local_max = jnp.max(logits, axis=0)
    raised = jnp.exp(logits - local_max)
    local_sum = jnp.sum(raised, axis=0)
    (raised,) = apart(raised)
    own_pair = jnp.stack([local_max, local_sum])
    turned = [own_pair] + [turn(own_pair, d) for d in range(1, peers)]

    def joined(a, b):
        top = jnp.maximum(a[0], b[0])
        return jnp.stack([top, a[1] * jnp.exp(a[0] - top) + b[1] * jnp.exp(b[0] - top)])

    both = turned[0]
    for other in turned[1:]:
        both = joined(both, other)
    for bit in bits_of(lines):
        both = joined(both, lax.ppermute(both, "cell", [(i, i ^ (bit * peers)) for i in range(n_cell)]))
    scales = [jnp.exp(t[0] - both[0]) / both[1] for t in turned]
    mapping = raised * scales[0]

    frame = spots + 2 * SIDE
    valid_all = spot_valid.astype(jnp.float32)
    nvalid = jnp.sum(valid_all)
    reach = SIDE + ROW + 1
    wide_valid = lax.dynamic_slice_in_dim(jnp.pad(valid_all, reach), offset, spots + 2 * reach)
    wide_slide = lax.dynamic_slice_in_dim(
        jnp.pad(slide_ids, reach, constant_values=-1), offset, spots + 2 * reach
    )
    up_spot = [(i, i + 1) for i in range(n_spot - 1)]
    down_spot = [(i + 1, i) for i in range(n_spot - 1)]

    def sides(tile):
        before = lax.ppermute(tile[:, -SIDE:], "spot", up_spot)
        after = lax.ppermute(tile[:, :SIDE], "spot", down_spot)
        return before, tile, after

    def framed(tile):
        return jnp.concatenate(sides(tile), axis=1)

    lists = framed(neighbours.T)
    spatial_wide = framed(spatial)
    spot_index = offset - SIDE + jnp.arange(frame, dtype=jnp.int32)
    inner = ROW + 1
    slide_frame = wide_slide[inner : inner + frame]
    valid_frame = wide_valid[inner : inner + frame]
    links = []
    for o in OFFSETS:
        listed = jnp.sum(((lists >= 0) & (lists == spot_index + o)).astype(jnp.float32), axis=0)
        there = wide_valid[inner + o : inner + o + frame] == 1.0
        same = wide_slide[inner + o : inner + o + frame] == slide_frame
        links.append(jnp.where(there & same, listed, 0.0))
    links = jnp.stack(links)
    counts = 1.0 + jnp.sum(links, axis=0)
    links, counts = apart(links, counts)
    valid_here = valid_frame[SIDE : SIDE + spots]
    slide_here = slide_frame[SIDE : SIDE + spots]
    members = (slide_here[None, :] == jnp.arange(SLIDES, dtype=jnp.int32)[:, None]).astype(jnp.float32)
    here, weighted = slice(SIDE, SIDE + spots), valid_here[None, :]
    early_sums = jnp.concatenate(
        [
            jnp.sum(members * (valid_here * density)[None, :], axis=1),
            jnp.sum(mapping * mapping * weighted)[None],
        ]
    )
    early_sums = all_sum(early_sums, "spot", bits_of(n_spot))
    target = density / jnp.sum(members * early_sums[:SLIDES, None], axis=0)
    frame_rows = jnp.stack([counts, valid_frame])
    gene_total = jnp.sum(genes_all, axis=1)
    ready = (links, frame_rows, spatial_wide, target, early_sums, gene_total, nvalid)

    def part(block, columns=None):
        columns = gene_block(block) if columns is None else columns
        return lax.dot_general(columns, raised, (((0,), (0,)), ((), ())), precision=highest)

    def line_pairs(pairs):
        return [(a * peers + c, b * peers + c) for a, b in pairs for c in range(peers)]

    def along(up_value, up_from, down_value, down_from):
        up_pairs = [(a, a + 1) for a in up_from]
        down_pairs = [(a, a - 1) for a in down_from]
        targets = {b for _, b in up_pairs} & {b for _, b in down_pairs}
        if targets or set(up_from) & set(down_from):
            return (
                lax.ppermute(up_value, "cell", line_pairs(up_pairs)),
                lax.ppermute(down_value, "cell", line_pairs(down_pairs)),
            )
        value = choose(z, [(up_value, list(up_from)), (down_value, list(down_from))])
        moved = lax.ppermute(value, "cell", line_pairs(up_pairs + down_pairs))
        return moved, moved

    if few_peers:
        units = []
        for u in range(lines):
            to = entry(z, [order[a][u] for a in range(lines)])
            sent = [turn(part(to * peers + (y + d) % peers, None if u else early[d]), d) for d in range(1, peers)]
            unit = part(to * peers + y) * scales[0]
            for value, scale in zip(sent, scales[1:]):
                unit = unit + value * scale
            units.append(unit)

        def unit_for(target):
            wanted = [[] for _ in range(lines)]
            for a in range(lines):
                if 0 <= target(a) < lines:
                    wanted[order[a].index(target(a))].append(a)
            return choose(z, list(zip(units, wanted)))

        got_up = got_down = None
        for p in range(lines - 1, 0, -1):
            up_value, down_value = unit_for(lambda a: a + p), unit_for(lambda a: a - p)
            if got_up is not None:
                up_value, down_value = up_value + got_up, down_value + got_down
            if p == 1:
                up_value, down_value, *ready = apart(up_value, down_value, *ready)
            got_up, got_down = along(up_value, range(0, lines - p), down_value, range(p, lines))
        predicted = unit_for(lambda a: a)
        if got_up is not None:
            predicted = predicted + got_up + got_down
    else:
        whole = lax.dot_general(genes_all, mapping, (((0,), (0,)), ((), ())), precision=highest)
        predicted = lax.psum_scatter(whole, "cell", scatter_dimension=0, tiled=True)

    links, frame_rows, spatial_wide, target, early_sums, gene_total, nvalid = ready
    smoothed_wide, spot_sums, gene_sums = smooth_call(links, frame_rows, *sides(predicted), spatial_wide)
    gene_sums = all_sum(gene_sums[:, :4].T, "spot", bits_of(n_spot))
    spot_sums = all_sum(spot_sums, "cell", bits_of(n_cell))
    gene_inner, gene_own, gene_target, pred_squares = (gene_sums[i] for i in range(4))
    spot_inner, spot_own, spot_target, row_sums = (spot_sums[i] for i in range(4))
    row_sums = row_sums[here]
    gene_scale = lax.rsqrt((gene_own + epsilon) * (gene_target + epsilon))
    spot_scale = lax.rsqrt((spot_own + epsilon) * (spot_target + epsilon))
    cos_gene = gene_inner * gene_scale
    cos_spot = (spot_inner * spot_scale)[here]
    by_gene = total_cells * gene_scale
    by_spot = total_cells * total_spots / nvalid * spot_scale
    frame_rows = jnp.stack([-valid_frame / counts, by_spot, spot_inner / (spot_own + epsilon)])
    gene_rows = jnp.stack([by_gene, gene_inner / (gene_own + epsilon)], axis=1)
    grad_pred, dots = spread_call(links, frame_rows, gene_rows, smoothed_wide, spatial_wide, predicted)

    kl_known = valid_here * target * (jnp.log(target) - jnp.log(row_sums))
    spot_part = jnp.concatenate(
        [
            jnp.sum(valid_here * cos_spot)[None],
            jnp.sum(kl_known)[None],
            jnp.sum(members * (valid_here * target)[None, :], axis=1),
            jnp.sum(members * (valid_here * row_sums)[None, :], axis=1),
        ]
    )
    spot_part = all_sum(spot_part, "spot", bits_of(n_spot))
    late = jnp.concatenate(
        [
            dots[0],
            jnp.sum(pred_squares)[None],
            early_sums[SLIDES:],
            jnp.sum(gene_own)[None],
            jnp.sum(cos_gene)[None],
        ]
    )
    late = all_sum(late, "cell", bits_of(n_cell))
    row_tot = spot_part[2 + SLIDES :]
    slide_rows = jnp.sum(members * row_tot[:, None], axis=0)
    level = total_cells * total_spots * valid_here * (1.0 / slide_rows - target / row_sums)
    column_dot = late[:spots] + level * row_sums
    (mapping,) = apart(mapping)
    share = all_sum(jnp.sum(mapping * level[None, :], axis=1), "spot", bits_of(n_spot))

    grad_map = None
    if few_peers:
        far = [sorted((t for t in range(lines)), key=lambda t: (abs(t - a), t)) for a in range(lines)]
        ups, downs = [grad_pred], [grad_pred]
        for p in range(1, lines):
            up, down = along(ups[-1], range(p - 1, lines - 1), downs[-1], range(1, lines - p + 1))
            ups.append(up)
            downs.append(down)
        slots = []
        for u in range(lines):
            options = [(grad_pred, [])] + [(v, []) for v in ups[1:]] + [(v, []) for v in downs[1:]]
            for a in range(lines):
                t = far[a][u]
                at = 0 if t == a else (a - t if t < a else lines - 1 + t - a)
                options[at][1].append(a)
            slots.append(choose(z, options))
            slots[u], *passed = apart(slots[u], *ups[1 : u + 1], *downs[1 : u + 1])
            ups[1 : u + 1], downs[1 : u + 1] = passed[:u], passed[u:]

        lines_at = [entry(z, [far[a][u] for a in range(lines)]) for u in range(lines)]
        waves = [[] for _ in range(lines + 1)]
        for u in range(lines):
            waves[u].append((u, 0, slots[u]))
            for d in range(1, peers):
                waves[u + 1].append((u, d, turn(slots[u], d)))
        kept = [None] * peers
        grad_expr = jnp.zeros((cells, gene_cols), jnp.float32)

        def placed(total, d):
            return lax.dynamic_update_slice_in_dim(total, kept[d] + share[:, None], ((y - d) % peers) * genes, axis=1)

        for w, wave in enumerate(waves):
            if w == lines:
                grad_expr = placed(grad_expr, 0)
                held_back = [kept[d] for d in range(1, peers)]
                blocks = [block for _, _, block in wave]
                tied = apart(grad_map, grad_expr, *held_back, *blocks)
                grad_map, grad_expr = tied[:2]
                kept[1:] = tied[2 : 1 + peers]
                wave = [(u, d, block) for (u, d, _), block in zip(wave, tied[1 + peers :])]
            for u, d, block in wave:
                to = lines_at[u]
                names = to * peers + (y - d) % peers
                wide_grad = lax.dot_general(mapping, block, (((1,), (1,)), ((), ())), precision=highest)
                for bit in bits_of(n_spot):
                    pairs = []
                    for i in range(n_cell):
                        t = far[i // peers][u]
                        for j in range(n_spot):
                            if (j ^ t) & (2 * bit - 1) == bit:
                                pairs.append((j * n_cell + i, (j ^ bit) * n_cell + i))
                    wide_grad = wide_grad + lax.ppermute(wide_grad, ("spot", "cell"), pairs)
                piece = jnp.dot(gene_block(names), block, precision=highest)
                grad_map = piece if grad_map is None else grad_map + piece
                kept[d] = wide_grad if kept[d] is None else jnp.where(s == to, wide_grad, kept[d])
        for d in range(1, peers):
            grad_expr = placed(grad_expr, d)
    else:
        rows = lax.all_gather(grad_pred, "cell", axis=0, tiled=True)
        grad_map = jnp.dot(genes_all, rows, precision=highest)
        wide_grad = lax.dot_general(mapping, rows, (((1,), (1,)), ((), ())), precision=highest)
        grad_expr = lax.psum_scatter(wide_grad, "spot", scatter_dimension=1, tiled=True) + share[:, None]
    grad_logits = mapping * (grad_map + (gene_total[:, None] * level[None, :] - column_dot[None, :]))

    pred_sq, map_sq, smooth_sq, cos_total = (late[spots + i] for i in range(4))
    gene_loss = 1.0 - cos_total / GENES
    spot_loss = 1.0 - spot_part[0] / nvalid
    density_loss = spot_part[1] + jnp.sum(jnp.where(row_tot > 0, spot_part[2 : 2 + SLIDES] * jnp.log(row_tot), 0.0))
    rms_weights = total_cells * jnp.sqrt(map_sq / (total_cells * nvalid))
    rms_pred = jnp.sqrt(pred_sq / (GENES * nvalid))
    rms_smooth = jnp.sqrt(smooth_sq / (GENES * nvalid))
    return (gene_loss, spot_loss, density_loss, grad_logits, grad_expr, rms_weights, rms_pred, rms_smooth)


def solution(mesh):
    placed = (
        P("cell", "spot"),
        P("cell", "spot"),
        P("cell", "spot"),
        P("spot"),
        P(),
        P(),
        P("spot", None),
    )
    step_map = jax.shard_map(
        step,
        mesh=mesh,
        in_specs=placed,
        out_specs=(P(), P(), P(), P("cell", "spot"), P("cell", "spot"), P(), P(), P()),
        check_vma=False,
    )
    if mesh.shape["cell"] > 2 * mesh.shape["spot"]:
        return step_map
    return step_map
```

```python
import jax
import jax.numpy as jnp
from jax import lax
from jax.experimental import pallas as pl
from jax.experimental.pallas import tpu as pltpu
from jax.sharding import PartitionSpec as P

GENES = 2048
ROW = 64
SLIDES = 3
SIDE = 2 * ROW
OFFSETS = (-ROW - 1, -ROW, -ROW + 1, -1, 1, ROW - 1, ROW, ROW + 1)

epsilon = 1e-06
highest = lax.Precision.HIGHEST


def apart(*values):
    return lax.optimization_barrier(values)


def bits_of(count):
    return [1 << b for b in range(count.bit_length() - 1)]


def all_sum(value, axis, bits):
    size = lax.axis_size(axis)
    for bit in bits:
        value = value + lax.ppermute(value, axis, [(i, i ^ bit) for i in range(size)])
    return value


def is_one_of(index, wanted):
    hit = index == wanted[0]
    for other in wanted[1:]:
        hit = hit | (index == other)
    return hit


def entry(index, values):
    picked = jnp.int32(values[0])
    for i, value in enumerate(values[1:], 1):
        picked = jnp.where(index == i, jnp.int32(value), picked)
    return picked


def choose(index, options):
    options = [o for o in options if o[1]]
    chosen = options[0][0]
    for value, wanted in options[1:]:
        chosen = jnp.where(is_one_of(index, wanted), value, chosen)
    return chosen


def smooth_kernel(links, rows, before, tile, after, spatial, smoothed, spot_sums, gene_sums):
    frame = spatial.shape[1]
    value = jnp.concatenate([before[...], tile[...], after[...]], axis=1)
    total = value
    for i, o in enumerate(OFFSETS):
        total = total + links[i : i + 1, :] * pltpu.roll(value, (-o) % frame, 1)
    smooth = total / rows[0:1, :]
    smoothed[...] = smooth
    there = spatial[...]
    inner, own = smooth * there, smooth * smooth

    @pl.when(pl.program_id(0) == 0)
    def _():
        spot_sums[...] = jnp.zeros_like(spot_sums)

    for i, part in enumerate((inner, own, there * there, value)):
        spot_sums[i : i + 1, :] += jnp.sum(part, axis=0, keepdims=True)
    here = slice(SIDE, frame - SIDE)
    valid = rows[1:2, here]
    lane = lax.broadcasted_iota(jnp.int32, gene_sums.shape, 1)
    sums = jnp.zeros(gene_sums.shape, jnp.float32)
    for i, part in enumerate((inner, own, there * there, value * value)):
        sums = jnp.where(lane == i, jnp.sum(valid * part[:, here], axis=1, keepdims=True), sums)
    gene_sums[...] = sums


def smooth_call(links, rows, before, tile, after, spatial):
    genes, frame = spatial.shape
    step = min(32, genes)
    whole = lambda a: pl.BlockSpec(a.shape, lambda i: (0, 0))
    some = lambda width: pl.BlockSpec((step, width), lambda i: (i, 0))
    return pl.pallas_call(
        smooth_kernel,
        grid=(genes // step,),
        in_specs=[whole(links), whole(rows), some(SIDE), some(tile.shape[1]), some(SIDE), some(frame)],
        out_specs=[some(frame), pl.BlockSpec((4, frame), lambda i: (0, 0)), some(128)],
        out_shape=[
            jax.ShapeDtypeStruct((genes, frame), jnp.float32),
            jax.ShapeDtypeStruct((4, frame), jnp.float32),
            jax.ShapeDtypeStruct((genes, 128), jnp.float32),
        ],
        name="smooth",
    )(links, rows, before, tile, after, spatial)


def step(logits, expression, spatial, density, slide_ids, spot_valid, neighbours):
    cells, spots = logits.shape
    genes = spatial.shape[0]
    gene_cols = expression.shape[1]
    n_spot, n_cell = lax.axis_size("spot"), lax.axis_size("cell")
    total_cells, total_spots = cells * n_cell, spots * n_spot
    lines, peers = n_spot, n_cell // n_spot
    few_peers = peers <= 2
    s = lax.axis_index("spot")
    k = lax.axis_index("cell")
    z, y = k // peers, k % peers
    offset = s * spots

    def turn(value, d):
        pairs = [(i, (i // peers) * peers + (i % peers + d) % peers) for i in range(n_cell)]
        return lax.ppermute(value, "cell", pairs)

    order = [sorted(range(lines), key=lambda t: (-abs(t - a), abs(2 * t - lines + 1))) for a in range(lines)]
    far_line = entry(z, [order[a][0] for a in range(lines)])
    early = {}
    for d in range(1, peers if few_peers else 1):
        value = lax.dynamic_slice_in_dim(expression, ((y + d) % peers) * genes, genes, axis=1)
        left = n_spot - 1
        for bit in reversed(bits_of(n_spot)):
            pairs = [
                (j * n_cell + i, (j ^ bit) * n_cell + i)
                for i in range(n_cell)
                for j in range(n_spot)
                if (j ^ order[i // peers][0]) & left == 0
            ]
            got = lax.ppermute(value, ("spot", "cell"), pairs)
            value = jnp.where(((s ^ far_line) & left) == bit, got, value)
            left -= bit
        early[d] = value

    held = {0: expression}
    for bit in reversed(bits_of(n_spot)):
        pairs = [(i, i ^ bit) for i in range(n_spot)]
        held.update({m ^ bit: lax.ppermute(v, "spot", pairs) for m, v in list(held.items())})
    genes_all = jnp.concatenate(
        [choose(s, [(held[m], [i for i in range(n_spot) if i ^ m == j]) for m in held]) for j in range(n_spot)],
        axis=1,
    )
    (genes_all,) = apart(genes_all)

    def gene_block(block):
        return lax.dynamic_slice_in_dim(genes_all, block * genes, genes, axis=1)

    raised = jnp.exp(logits)
    local_sum = jnp.sum(raised, axis=0)
    (raised,) = apart(raised)
    column_sum = all_sum(local_sum, "cell", bits_of(n_cell))
    mapping = raised / column_sum

    frame = spots + 2 * SIDE
    valid_all = spot_valid.astype(jnp.float32)
    nvalid = jnp.sum(valid_all)
    reach = SIDE + ROW + 1
    wide_valid = lax.dynamic_slice_in_dim(jnp.pad(valid_all, reach), offset, spots + 2 * reach)
    wide_slide = lax.dynamic_slice_in_dim(
        jnp.pad(slide_ids, reach, constant_values=-1), offset, spots + 2 * reach
    )
    up_spot = [(i, i + 1) for i in range(n_spot - 1)]
    down_spot = [(i + 1, i) for i in range(n_spot - 1)]

    def sides(tile):
        before = lax.ppermute(tile[:, -SIDE:], "spot", up_spot)
        after = lax.ppermute(tile[:, :SIDE], "spot", down_spot)
        return before, tile, after

    def framed(tile):
        return jnp.concatenate(sides(tile), axis=1)

    lists = framed(neighbours.T)
    spatial_wide = framed(spatial)
    spot_index = offset - SIDE + jnp.arange(frame, dtype=jnp.int32)
    inner = ROW + 1
    slide_frame = wide_slide[inner : inner + frame]
    valid_frame = wide_valid[inner : inner + frame]
    links = []
    for o in OFFSETS:
        listed = jnp.sum(((lists >= 0) & (lists == spot_index + o)).astype(jnp.float32), axis=0)
        there = wide_valid[inner + o : inner + o + frame] == 1.0
        same = wide_slide[inner + o : inner + o + frame] == slide_frame
        links.append(jnp.where(there & same, listed, 0.0))
    links = jnp.stack(links)
    counts = 1.0 + jnp.sum(links, axis=0)
    links, counts = apart(links, counts)
    valid_here = valid_frame[SIDE : SIDE + spots]
    slide_here = slide_frame[SIDE : SIDE + spots]
    members = (slide_here[None, :] == jnp.arange(SLIDES, dtype=jnp.int32)[:, None]).astype(jnp.float32)
    here, weighted = slice(SIDE, SIDE + spots), valid_here[None, :]
    early_sums = jnp.concatenate(
        [
            jnp.sum(members * (valid_here * density)[None, :], axis=1),
            jnp.sum(mapping * mapping * weighted)[None],
        ]
    )
    early_sums = all_sum(early_sums, "spot", bits_of(n_spot))
    target = density / jnp.sum(members * early_sums[:SLIDES, None], axis=0)
    frame_rows = jnp.stack([counts, valid_frame])
    gene_total = jnp.sum(genes_all, axis=1)
    ready = (links, frame_rows, spatial_wide, target, early_sums, gene_total, nvalid)

    def part(block, columns=None):
        columns = gene_block(block) if columns is None else columns
        return lax.dot_general(columns, raised, (((0,), (0,)), ((), ())), precision=highest)

    def line_pairs(pairs):
        return [(a * peers + c, b * peers + c) for a, b in pairs for c in range(peers)]

    def along(up_value, up_from, down_value, down_from):
        up_pairs = [(a, a + 1) for a in up_from]
        down_pairs = [(a, a - 1) for a in down_from]
        targets = {b for _, b in up_pairs} & {b for _, b in down_pairs}
        if targets or set(up_from) & set(down_from):
            return (
                lax.ppermute(up_value, "cell", line_pairs(up_pairs)),
                lax.ppermute(down_value, "cell", line_pairs(down_pairs)),
            )
        value = choose(z, [(up_value, list(up_from)), (down_value, list(down_from))])
        moved = lax.ppermute(value, "cell", line_pairs(up_pairs + down_pairs))
        return moved, moved

    if few_peers:
        units = []
        for u in range(lines):
            to = entry(z, [order[a][u] for a in range(lines)])
            sent = [turn(part(to * peers + (y + d) % peers, None if u else early[d]), d) for d in range(1, peers)]
            (unit,) = apart(part(to * peers + y))
            for value in sent:
                unit = unit + value
            units.append(unit)

        def unit_for(target):
            wanted = [[] for _ in range(lines)]
            for a in range(lines):
                if 0 <= target(a) < lines:
                    wanted[order[a].index(target(a))].append(a)
            return choose(z, list(zip(units, wanted)))

        got_up = got_down = None
        for p in range(lines - 1, 0, -1):
            up_value, down_value = unit_for(lambda a: a + p), unit_for(lambda a: a - p)
            if got_up is not None:
                up_value, down_value = up_value + got_up, down_value + got_down
            if p == 1:
                up_value, down_value, *ready = apart(up_value, down_value, *ready)
            got_up, got_down = along(up_value, range(0, lines - p), down_value, range(p, lines))
        predicted = unit_for(lambda a: a)
        if got_up is not None:
            predicted = predicted + got_up + got_down
        predicted = predicted / column_sum
    else:
        whole = lax.dot_general(genes_all, mapping, (((0,), (0,)), ((), ())), precision=highest)
        predicted = lax.psum_scatter(whole, "cell", scatter_dimension=0, tiled=True)

    links, frame_rows, spatial_wide, target, early_sums, gene_total, nvalid = ready
    smoothed_wide, spot_sums, gene_sums = smooth_call(links, frame_rows, *sides(predicted), spatial_wide)
    gene_sums = all_sum(gene_sums[:, :4].T, "spot", bits_of(n_spot))
    spot_sums = all_sum(spot_sums, "cell", bits_of(n_cell))
    gene_inner, gene_own, gene_target, pred_squares = (gene_sums[i] for i in range(4))
    spot_inner, spot_own, spot_target, row_sums = (spot_sums[i] for i in range(4))
    row_sums = row_sums[here]
    gene_scale = lax.rsqrt((gene_own + epsilon) * (gene_target + epsilon))
    spot_scale = lax.rsqrt((spot_own + epsilon) * (spot_target + epsilon))
    cos_gene = gene_inner * gene_scale
    cos_spot = (spot_inner * spot_scale)[here]
    by_gene = total_cells * gene_scale
    by_spot = total_cells * total_spots / nvalid * spot_scale
    spread_in = (
        -valid_frame
        / counts
        * (
            (spatial_wide - (gene_inner / (gene_own + epsilon))[:, None] * smoothed_wide) * by_gene[:, None]
            + (spatial_wide - (spot_inner / (spot_own + epsilon))[None, :] * smoothed_wide) * by_spot[None, :]
        )
    )
    (spread_in,) = apart(spread_in)

    def shifted(value, o):
        return jnp.pad(value, ((0, 0), (ROW + 1, ROW + 1)))[:, ROW + 1 + o : ROW + 1 + o + frame]

    spread = spread_in
    for i, o in enumerate(OFFSETS):
        spread = spread + shifted(links[i] * spread_in, -o)
    grad_pred = spread[:, here]
    (grad_pred,) = apart(grad_pred)

    kl_known = valid_here * target * (jnp.log(target) - jnp.log(row_sums))
    spot_part = jnp.concatenate(
        [
            jnp.sum(valid_here * cos_spot)[None],
            jnp.sum(kl_known)[None],
            jnp.sum(members * (valid_here * target)[None, :], axis=1),
            jnp.sum(members * (valid_here * row_sums)[None, :], axis=1),
        ]
    )
    spot_part = all_sum(spot_part, "spot", bits_of(n_spot))
    late = jnp.concatenate(
        [
            jnp.sum(predicted * grad_pred, axis=0),
            jnp.sum(pred_squares)[None],
            early_sums[SLIDES:],
            jnp.sum(gene_own)[None],
            jnp.sum(cos_gene)[None],
        ]
    )
    late = all_sum(late, "cell", bits_of(n_cell))
    row_tot = spot_part[2 + SLIDES :]
    slide_rows = jnp.sum(members * row_tot[:, None], axis=0)
    level = total_cells * total_spots * valid_here * (1.0 / slide_rows - target / row_sums)
    column_dot = late[:spots] + level * row_sums
    (mapping,) = apart(mapping)
    share = all_sum(jnp.sum(mapping * level[None, :], axis=1), "spot", bits_of(n_spot))

    grad_map = None
    if few_peers:
        far = [sorted((t for t in range(lines)), key=lambda t: (abs(t - a), t)) for a in range(lines)]
        ups, downs = [grad_pred], [grad_pred]
        for p in range(1, lines):
            up, down = along(ups[-1], range(p - 1, lines - 1), downs[-1], range(1, lines - p + 1))
            ups.append(up)
            downs.append(down)
        slots = []
        for u in range(lines):
            options = [(grad_pred, [])] + [(v, []) for v in ups[1:]] + [(v, []) for v in downs[1:]]
            for a in range(lines):
                t = far[a][u]
                at = 0 if t == a else (a - t if t < a else lines - 1 + t - a)
                options[at][1].append(a)
            slots.append(choose(z, options))
            slots[u], *passed = apart(slots[u], *ups[1 : u + 1], *downs[1 : u + 1])
            ups[1 : u + 1], downs[1 : u + 1] = passed[:u], passed[u:]

        lines_at = [entry(z, [far[a][u] for a in range(lines)]) for u in range(lines)]
        waves = [[] for _ in range(lines + 1)]
        for u in range(lines):
            waves[u].append((u, 0, slots[u]))
            for d in range(1, peers):
                waves[u + 1].append((u, d, turn(slots[u], d)))
        kept = [None] * peers
        grad_expr = jnp.zeros((cells, gene_cols), jnp.float32)

        def placed(total, d):
            return lax.dynamic_update_slice_in_dim(total, kept[d] + share[:, None], ((y - d) % peers) * genes, axis=1)

        for w, wave in enumerate(waves):
            if w == lines:
                grad_expr = placed(grad_expr, 0)
                held_back = [kept[d] for d in range(1, peers)]
                blocks = [block for _, _, block in wave]
                tied = apart(grad_map, grad_expr, *held_back, *blocks)
                grad_map, grad_expr = tied[:2]
                kept[1:] = tied[2 : 1 + peers]
                wave = [(u, d, block) for (u, d, _), block in zip(wave, tied[1 + peers :])]
            for u, d, block in wave:
                to = lines_at[u]
                names = to * peers + (y - d) % peers
                wide_grad = lax.dot_general(mapping, block, (((1,), (1,)), ((), ())), precision=highest)
                for bit in bits_of(n_spot):
                    pairs = []
                    for i in range(n_cell):
                        t = far[i // peers][u]
                        for j in range(n_spot):
                            if (j ^ t) & (2 * bit - 1) == bit:
                                pairs.append((j * n_cell + i, (j ^ bit) * n_cell + i))
                    wide_grad = wide_grad + lax.ppermute(wide_grad, ("spot", "cell"), pairs)
                piece = jnp.dot(gene_block(names), block, precision=highest)
                grad_map = piece if grad_map is None else grad_map + piece
                kept[d] = wide_grad if kept[d] is None else jnp.where(s == to, wide_grad, kept[d])
        for d in range(1, peers):
            grad_expr = placed(grad_expr, d)
    else:
        rows = lax.all_gather(grad_pred, "cell", axis=0, tiled=True)
        grad_map = jnp.dot(genes_all, rows, precision=highest)
        wide_grad = lax.dot_general(mapping, rows, (((1,), (1,)), ((), ())), precision=highest)
        grad_expr = lax.psum_scatter(wide_grad, "spot", scatter_dimension=1, tiled=True) + share[:, None]
    grad_logits = mapping * (grad_map + (gene_total[:, None] * level[None, :] - column_dot[None, :]))

    pred_sq, map_sq, smooth_sq, cos_total = (late[spots + i] for i in range(4))
    gene_loss = 1.0 - cos_total / GENES
    spot_loss = 1.0 - spot_part[0] / nvalid
    density_loss = spot_part[1] + jnp.sum(jnp.where(row_tot > 0, spot_part[2 : 2 + SLIDES] * jnp.log(row_tot), 0.0))
    rms_weights = total_cells * jnp.sqrt(map_sq / (total_cells * nvalid))
    rms_pred = jnp.sqrt(pred_sq / (GENES * nvalid))
    rms_smooth = jnp.sqrt(smooth_sq / (GENES * nvalid))
    return (gene_loss, spot_loss, density_loss, grad_logits, grad_expr, rms_weights, rms_pred, rms_smooth)


def solution(mesh):
    placed = (
        P("cell", "spot"),
        P("cell", "spot"),
        P("cell", "spot"),
        P("spot"),
        P(),
        P(),
        P("spot", None),
    )
    step_map = jax.shard_map(
        step,
        mesh=mesh,
        in_specs=placed,
        out_specs=(P(), P(), P(), P("cell", "spot"), P("cell", "spot"), P(), P(), P()),
        check_vma=False,
    )
    if mesh.shape["cell"] > 2 * mesh.shape["spot"]:
        return step_map
    return step_map
```

```python
import jax
import jax.numpy as jnp
from jax import lax
from jax.experimental import pallas as pl
from jax.experimental.pallas import tpu as pltpu
from jax.sharding import PartitionSpec as P

GENES = 2048
ROW = 64
SLIDES = 3
SIDE = 2 * ROW
OFFSETS = (-ROW - 1, -ROW, -ROW + 1, -1, 1, ROW - 1, ROW, ROW + 1)

epsilon = 1e-06
highest = lax.Precision.HIGHEST


def apart(*values):
    return lax.optimization_barrier(values)


def bits_of(count):
    return [1 << b for b in range(count.bit_length() - 1)]


def all_sum(value, axis, bits):
    size = lax.axis_size(axis)
    for bit in bits:
        value = value + lax.ppermute(value, axis, [(i, i ^ bit) for i in range(size)])
    return value


def is_one_of(index, wanted):
    hit = index == wanted[0]
    for other in wanted[1:]:
        hit = hit | (index == other)
    return hit


def entry(index, values):
    picked = jnp.int32(values[0])
    for i, value in enumerate(values[1:], 1):
        picked = jnp.where(index == i, jnp.int32(value), picked)
    return picked


def choose(index, options):
    options = [o for o in options if o[1]]
    chosen = options[0][0]
    for value, wanted in options[1:]:
        chosen = jnp.where(is_one_of(index, wanted), value, chosen)
    return chosen


def smooth_kernel(links, rows, before, tile, after, spatial, smoothed, spot_sums, gene_sums):
    frame = spatial.shape[1]
    value = jnp.concatenate([before[...], tile[...], after[...]], axis=1)
    total = value
    for i, o in enumerate(OFFSETS):
        total = total + links[i : i + 1, :] * pltpu.roll(value, (-o) % frame, 1)
    smooth = total / rows[0:1, :]
    smoothed[...] = smooth
    there = spatial[...]
    inner, own = smooth * there, smooth * smooth

    @pl.when(pl.program_id(0) == 0)
    def _():
        spot_sums[...] = jnp.zeros_like(spot_sums)

    for i, part in enumerate((inner, own, there * there, value)):
        spot_sums[i : i + 1, :] += jnp.sum(part, axis=0, keepdims=True)
    here = slice(SIDE, frame - SIDE)
    valid = rows[1:2, here]
    lane = lax.broadcasted_iota(jnp.int32, gene_sums.shape, 1)
    sums = jnp.zeros(gene_sums.shape, jnp.float32)
    for i, part in enumerate((inner, own, there * there, value * value)):
        sums = jnp.where(lane == i, jnp.sum(valid * part[:, here], axis=1, keepdims=True), sums)
    gene_sums[...] = sums


def smooth_call(links, rows, before, tile, after, spatial):
    genes, frame = spatial.shape
    step = min(32, genes)
    whole = lambda a: pl.BlockSpec(a.shape, lambda i: (0, 0))
    some = lambda width: pl.BlockSpec((step, width), lambda i: (i, 0))
    return pl.pallas_call(
        smooth_kernel,
        grid=(genes // step,),
        in_specs=[whole(links), whole(rows), some(SIDE), some(tile.shape[1]), some(SIDE), some(frame)],
        out_specs=[some(frame), pl.BlockSpec((4, frame), lambda i: (0, 0)), some(128)],
        out_shape=[
            jax.ShapeDtypeStruct((genes, frame), jnp.float32),
            jax.ShapeDtypeStruct((4, frame), jnp.float32),
            jax.ShapeDtypeStruct((genes, 128), jnp.float32),
        ],
        name="smooth",
    )(links, rows, before, tile, after, spatial)


def step(logits, expression, spatial, density, slide_ids, spot_valid, neighbours):
    cells, spots = logits.shape
    genes = spatial.shape[0]
    gene_cols = expression.shape[1]
    n_spot, n_cell = lax.axis_size("spot"), lax.axis_size("cell")
    total_cells, total_spots = cells * n_cell, spots * n_spot
    lines, peers = n_spot, n_cell // n_spot
    few_peers = peers <= 2
    s = lax.axis_index("spot")
    k = lax.axis_index("cell")
    z, y = k // peers, k % peers
    offset = s * spots

    def turn(value, d):
        pairs = [(i, (i // peers) * peers + (i % peers + d) % peers) for i in range(n_cell)]
        return lax.ppermute(value, "cell", pairs)

    order = [sorted(range(lines), key=lambda t: (-abs(t - a), abs(2 * t - lines + 1))) for a in range(lines)]
    far_line = entry(z, [order[a][0] for a in range(lines)])
    early = {}
    for d in range(1, peers if few_peers else 1):
        value = lax.dynamic_slice_in_dim(expression, ((y + d) % peers) * genes, genes, axis=1)
        left = n_spot - 1
        for bit in reversed(bits_of(n_spot)):
            pairs = [
                (j * n_cell + i, (j ^ bit) * n_cell + i)
                for i in range(n_cell)
                for j in range(n_spot)
                if (j ^ order[i // peers][0]) & left == 0
            ]
            got = lax.ppermute(value, ("spot", "cell"), pairs)
            value = jnp.where(((s ^ far_line) & left) == bit, got, value)
            left -= bit
        early[d] = value

    held = {0: expression}
    for bit in reversed(bits_of(n_spot)):
        pairs = [(i, i ^ bit) for i in range(n_spot)]
        held.update({m ^ bit: lax.ppermute(v, "spot", pairs) for m, v in list(held.items())})
    genes_all = jnp.concatenate(
        [choose(s, [(held[m], [i for i in range(n_spot) if i ^ m == j]) for m in held]) for j in range(n_spot)],
        axis=1,
    )
    (genes_all,) = apart(genes_all)

    def gene_block(block):
        return lax.dynamic_slice_in_dim(genes_all, block * genes, genes, axis=1)

    raised = jnp.exp(logits)
    local_sum = jnp.sum(raised, axis=0)
    (raised,) = apart(raised)
    column_sum = all_sum(local_sum, "cell", bits_of(n_cell))
    mapping = raised / column_sum

    frame = spots + 2 * SIDE
    valid_all = spot_valid.astype(jnp.float32)
    nvalid = jnp.sum(valid_all)
    reach = SIDE + ROW + 1
    wide_valid = lax.dynamic_slice_in_dim(jnp.pad(valid_all, reach), offset, spots + 2 * reach)
    wide_slide = lax.dynamic_slice_in_dim(
        jnp.pad(slide_ids, reach, constant_values=-1), offset, spots + 2 * reach
    )
    up_spot = [(i, i + 1) for i in range(n_spot - 1)]
    down_spot = [(i + 1, i) for i in range(n_spot - 1)]

    def sides(tile):
        before = lax.ppermute(tile[:, -SIDE:], "spot", up_spot)
        after = lax.ppermute(tile[:, :SIDE], "spot", down_spot)
        return before, tile, after

    def framed(tile):
        return jnp.concatenate(sides(tile), axis=1)

    lists = framed(neighbours.T)
    spatial_wide = framed(spatial)
    spot_index = offset - SIDE + jnp.arange(frame, dtype=jnp.int32)
    inner = ROW + 1
    slide_frame = wide_slide[inner : inner + frame]
    valid_frame = wide_valid[inner : inner + frame]
    links = []
    for o in OFFSETS:
        listed = jnp.sum(((lists >= 0) & (lists == spot_index + o)).astype(jnp.float32), axis=0)
        there = wide_valid[inner + o : inner + o + frame] == 1.0
        same = wide_slide[inner + o : inner + o + frame] == slide_frame
        links.append(jnp.where(there & same, listed, 0.0))
    links = jnp.stack(links)
    counts = 1.0 + jnp.sum(links, axis=0)
    links, counts = apart(links, counts)
    valid_here = valid_frame[SIDE : SIDE + spots]
    slide_here = slide_frame[SIDE : SIDE + spots]
    members = (slide_here[None, :] == jnp.arange(SLIDES, dtype=jnp.int32)[:, None]).astype(jnp.float32)
    here, weighted = slice(SIDE, SIDE + spots), valid_here[None, :]
    early_sums = jnp.concatenate(
        [
            jnp.sum(members * (valid_here * density)[None, :], axis=1),
            jnp.sum(mapping * mapping * weighted)[None],
        ]
    )
    early_sums = all_sum(early_sums, "spot", bits_of(n_spot))
    target = density / jnp.sum(members * early_sums[:SLIDES, None], axis=0)
    frame_rows = jnp.stack([counts, valid_frame])
    gene_total = jnp.sum(genes_all, axis=1)
    ready = (links, frame_rows, spatial_wide, target, early_sums, gene_total, nvalid)

    def part(block, columns=None):
        columns = gene_block(block) if columns is None else columns
        return lax.dot_general(columns, raised, (((0,), (0,)), ((), ())), precision=highest)

    def line_pairs(pairs):
        return [(a * peers + c, b * peers + c) for a, b in pairs for c in range(peers)]

    def along(near_value, far_value, up_from, down_from):
        hops = [(a, a + 1) for a in up_from] + [(a, a - 1) for a in down_from]
        links_of = [[hop for hop in hops if min(hop) % 2 == parity] for parity in range(2)]
        return [
            lax.ppermute(value, "cell", line_pairs(pairs)) if pairs else jnp.zeros_like(value)
            for value, pairs in zip((near_value, far_value), links_of)
        ]

    if few_peers:
        units = []
        for u in range(lines):
            to = entry(z, [order[a][u] for a in range(lines)])
            sent = [turn(part(to * peers + (y + d) % peers, None if u else early[d]), d) for d in range(1, peers)]
            (unit,) = apart(part(to * peers + y))
            for value in sent:
                unit = unit + value
            units.append(unit)

        def unit_for(target):
            wanted = [[] for _ in range(lines)]
            for a in range(lines):
                if 0 <= target(a) < lines:
                    wanted[order[a].index(target(a))].append(a)
            return choose(z, list(zip(units, wanted))) if any(wanted) else jnp.zeros_like(units[0])

        got_even = got_odd = None
        for p in range(lines - 1, 0, -1):
            even_value = unit_for(lambda a: a + p if a % 2 == 0 else a - p)
            odd_value = unit_for(lambda a: a - p if a % 2 == 0 else a + p)
            if got_even is not None:
                even_value, odd_value = even_value + got_odd, odd_value + got_even
            if p == 1:
                even_value, odd_value, *ready = apart(even_value, odd_value, *ready)
            got_even, got_odd = along(even_value, odd_value, range(0, lines - p), range(p, lines))
        predicted = unit_for(lambda a: a)
        if got_even is not None:
            predicted = predicted + got_even + got_odd
        predicted = predicted / column_sum
    else:
        whole = lax.dot_general(genes_all, mapping, (((0,), (0,)), ((), ())), precision=highest)
        predicted = lax.psum_scatter(whole, "cell", scatter_dimension=0, tiled=True)

    links, frame_rows, spatial_wide, target, early_sums, gene_total, nvalid = ready
    smoothed_wide, spot_sums, gene_sums = smooth_call(links, frame_rows, *sides(predicted), spatial_wide)
    gene_sums = all_sum(gene_sums[:, :4].T, "spot", bits_of(n_spot))
    spot_sums = all_sum(spot_sums, "cell", bits_of(n_cell))
    gene_inner, gene_own, gene_target, pred_squares = (gene_sums[i] for i in range(4))
    spot_inner, spot_own, spot_target, row_sums = (spot_sums[i] for i in range(4))
    row_sums = row_sums[here]
    gene_scale = lax.rsqrt((gene_own + epsilon) * (gene_target + epsilon))
    spot_scale = lax.rsqrt((spot_own + epsilon) * (spot_target + epsilon))
    cos_gene = gene_inner * gene_scale
    cos_spot = (spot_inner * spot_scale)[here]
    by_gene = total_cells * gene_scale
    by_spot = total_cells * total_spots / nvalid * spot_scale
    spread_in = (
        -valid_frame
        / counts
        * (
            (spatial_wide - (gene_inner / (gene_own + epsilon))[:, None] * smoothed_wide) * by_gene[:, None]
            + (spatial_wide - (spot_inner / (spot_own + epsilon))[None, :] * smoothed_wide) * by_spot[None, :]
        )
    )
    (spread_in,) = apart(spread_in)

    def shifted(value, o):
        return jnp.pad(value, ((0, 0), (ROW + 1, ROW + 1)))[:, ROW + 1 + o : ROW + 1 + o + frame]

    spread = spread_in
    for i, o in enumerate(OFFSETS):
        spread = spread + shifted(links[i] * spread_in, -o)
    grad_pred = spread[:, here]
    (grad_pred,) = apart(grad_pred)

    kl_known = valid_here * target * (jnp.log(target) - jnp.log(row_sums))
    spot_part = jnp.concatenate(
        [
            jnp.sum(valid_here * cos_spot)[None],
            jnp.sum(kl_known)[None],
            jnp.sum(members * (valid_here * target)[None, :], axis=1),
            jnp.sum(members * (valid_here * row_sums)[None, :], axis=1),
        ]
    )
    spot_part = all_sum(spot_part, "spot", bits_of(n_spot))
    late = jnp.concatenate(
        [
            jnp.sum(predicted * grad_pred, axis=0),
            jnp.sum(pred_squares)[None],
            early_sums[SLIDES:],
            jnp.sum(gene_own)[None],
            jnp.sum(cos_gene)[None],
        ]
    )
    late = all_sum(late, "cell", bits_of(n_cell))
    row_tot = spot_part[2 + SLIDES :]
    slide_rows = jnp.sum(members * row_tot[:, None], axis=0)
    level = total_cells * total_spots * valid_here * (1.0 / slide_rows - target / row_sums)
    column_dot = late[:spots] + level * row_sums
    (mapping,) = apart(mapping)
    share = all_sum(jnp.sum(mapping * level[None, :], axis=1), "spot", bits_of(n_spot))

    pred_sq, map_sq, smooth_sq, cos_total = (late[spots + i] for i in range(4))
    gene_loss = 1.0 - cos_total / GENES
    spot_loss = 1.0 - spot_part[0] / nvalid
    density_loss = spot_part[1] + jnp.sum(jnp.where(row_tot > 0, spot_part[2 : 2 + SLIDES] * jnp.log(row_tot), 0.0))
    rms_weights = total_cells * jnp.sqrt(map_sq / (total_cells * nvalid))
    rms_pred = jnp.sqrt(pred_sq / (GENES * nvalid))
    rms_smooth = jnp.sqrt(smooth_sq / (GENES * nvalid))
    losses = (gene_loss, spot_loss, density_loss, rms_weights, rms_pred, rms_smooth)

    grad_map = None
    if few_peers:
        far = [sorted((t for t in range(lines)), key=lambda t: (abs(t - a), t)) for a in range(lines)]
        evens, odds = [grad_pred], [grad_pred]
        for p in range(1, lines):
            even, odd = along(odds[-1], evens[-1], range(p - 1, lines - 1), range(1, lines - p + 1))
            evens.append(even)
            odds.append(odd)
        slots = []
        for u in range(lines):
            options = [(grad_pred, [])] + [(v, []) for v in evens[1:]] + [(v, []) for v in odds[1:]]
            for a in range(lines):
                t = far[a][u]
                from_even = (a % 2 == 0) == (t > a)
                at = 0 if t == a else abs(a - t) + (0 if from_even else lines - 1)
                options[at][1].append(a)
            slots.append(choose(z, options))
            slots[u], *passed = apart(slots[u], *evens[1 : u + 1], *odds[1 : u + 1])
            evens[1 : u + 1], odds[1 : u + 1] = passed[:u], passed[u:]

        lines_at = [entry(z, [far[a][u] for a in range(lines)]) for u in range(lines)]
        waves = [[] for _ in range(lines + 1)]
        for u in range(lines):
            waves[u].append((u, 0, slots[u]))
            for d in range(1, peers):
                waves[u + 1].append((u, d, turn(slots[u], d)))
        kept = [None] * peers
        grad_expr = jnp.zeros((cells, gene_cols), jnp.float32)

        def placed(total, d):
            return lax.dynamic_update_slice_in_dim(total, kept[d] + share[:, None], ((y - d) % peers) * genes, axis=1)

        for w, wave in enumerate(waves):
            if w == lines:
                grad_expr = placed(grad_expr, 0)
                held_back = [kept[d] for d in range(1, peers)]
                blocks = [block for _, _, block in wave]
                *tied, losses = apart(grad_map, grad_expr, *held_back, *blocks, losses)
                grad_map, grad_expr = tied[:2]
                kept[1:] = tied[2 : 1 + peers]
                wave = [(u, d, block) for (u, d, _), block in zip(wave, tied[1 + peers :])]
            for u, d, block in wave:
                to = lines_at[u]
                names = to * peers + (y - d) % peers
                wide_grad = lax.dot_general(mapping, block, (((1,), (1,)), ((), ())), precision=highest)
                for bit in bits_of(n_spot):
                    pairs = []
                    for i in range(n_cell):
                        t = far[i // peers][u]
                        for j in range(n_spot):
                            if (j ^ t) & (2 * bit - 1) == bit:
                                pairs.append((j * n_cell + i, (j ^ bit) * n_cell + i))
                    wide_grad = wide_grad + lax.ppermute(wide_grad, ("spot", "cell"), pairs)
                piece = jnp.dot(gene_block(names), block, precision=highest)
                grad_map = piece if grad_map is None else grad_map + piece
                kept[d] = wide_grad if kept[d] is None else jnp.where(s == to, wide_grad, kept[d])
        for d in range(1, peers):
            grad_expr = placed(grad_expr, d)
    else:
        rows = lax.all_gather(grad_pred, "cell", axis=0, tiled=True)
        grad_map = jnp.dot(genes_all, rows, precision=highest)
        wide_grad = lax.dot_general(mapping, rows, (((1,), (1,)), ((), ())), precision=highest)
        grad_expr = lax.psum_scatter(wide_grad, "spot", scatter_dimension=1, tiled=True) + share[:, None]
    grad_logits = mapping * (grad_map + (gene_total[:, None] * level[None, :] - column_dot[None, :]))

    return (*losses[:3], grad_logits, grad_expr, *losses[3:])


def solution(mesh):
    placed = (
        P("cell", "spot"),
        P("cell", "spot"),
        P("cell", "spot"),
        P("spot"),
        P(),
        P(),
        P("spot", None),
    )
    step_map = jax.shard_map(
        step,
        mesh=mesh,
        in_specs=placed,
        out_specs=(P(), P(), P(), P("cell", "spot"), P("cell", "spot"), P(), P(), P()),
        check_vma=False,
    )
    if mesh.shape["cell"] > 2 * mesh.shape["spot"]:
        return step_map
    return step_map
```

```python
import jax
import jax.numpy as jnp
from jax import lax
from jax.experimental import pallas as pl
from jax.experimental.pallas import tpu as pltpu
from jax.sharding import PartitionSpec as P

GENES = 2048
ROW = 64
SLIDES = 3
SIDE = 2 * ROW
OFFSETS = (-ROW - 1, -ROW, -ROW + 1, -1, 1, ROW - 1, ROW, ROW + 1)

epsilon = 1e-06
highest = lax.Precision.HIGHEST


def apart(*values):
    return lax.optimization_barrier(values)


def bits_of(count):
    return [1 << b for b in range(count.bit_length() - 1)]


def all_sum(value, axis, bits):
    size = lax.axis_size(axis)
    for bit in bits:
        value = value + lax.ppermute(value, axis, [(i, i ^ bit) for i in range(size)])
    return value


def is_one_of(index, wanted):
    hit = index == wanted[0]
    for other in wanted[1:]:
        hit = hit | (index == other)
    return hit


def entry(index, values):
    picked = jnp.int32(values[0])
    for i, value in enumerate(values[1:], 1):
        picked = jnp.where(index == i, jnp.int32(value), picked)
    return picked


def choose(index, options):
    options = [o for o in options if o[1]]
    chosen = options[0][0]
    for value, wanted in options[1:]:
        chosen = jnp.where(is_one_of(index, wanted), value, chosen)
    return chosen


def smooth_kernel(links, rows, before, tile, after, spatial, smoothed, spot_sums, gene_sums):
    frame = spatial.shape[1]
    value = jnp.concatenate([before[...], tile[...], after[...]], axis=1)
    total = value
    for i, o in enumerate(OFFSETS):
        total = total + links[i : i + 1, :] * pltpu.roll(value, (-o) % frame, 1)
    smooth = total / rows[0:1, :]
    smoothed[...] = smooth
    there = spatial[...]
    inner, own = smooth * there, smooth * smooth

    @pl.when(pl.program_id(0) == 0)
    def _():
        spot_sums[...] = jnp.zeros_like(spot_sums)

    for i, part in enumerate((inner, own, there * there, value)):
        spot_sums[i : i + 1, :] += jnp.sum(part, axis=0, keepdims=True)
    here = slice(SIDE, frame - SIDE)
    valid = rows[1:2, here]
    lane = lax.broadcasted_iota(jnp.int32, gene_sums.shape, 1)
    sums = jnp.zeros(gene_sums.shape, jnp.float32)
    for i, part in enumerate((inner, own, there * there, value * value)):
        sums = jnp.where(lane == i, jnp.sum(valid * part[:, here], axis=1, keepdims=True), sums)
    gene_sums[...] = sums


def smooth_call(links, rows, before, tile, after, spatial):
    genes, frame = spatial.shape
    step = min(32, genes)
    whole = lambda a: pl.BlockSpec(a.shape, lambda i: (0, 0))
    some = lambda width: pl.BlockSpec((step, width), lambda i: (i, 0))
    return pl.pallas_call(
        smooth_kernel,
        grid=(genes // step,),
        in_specs=[whole(links), whole(rows), some(SIDE), some(tile.shape[1]), some(SIDE), some(frame)],
        out_specs=[some(frame), pl.BlockSpec((4, frame), lambda i: (0, 0)), some(128)],
        out_shape=[
            jax.ShapeDtypeStruct((genes, frame), jnp.float32),
            jax.ShapeDtypeStruct((4, frame), jnp.float32),
            jax.ShapeDtypeStruct((genes, 128), jnp.float32),
        ],
        name="smooth",
    )(links, rows, before, tile, after, spatial)


def step(logits, expression, spatial, density, slide_ids, spot_valid, neighbours):
    cells, spots = logits.shape
    genes = spatial.shape[0]
    gene_cols = expression.shape[1]
    n_spot, n_cell = lax.axis_size("spot"), lax.axis_size("cell")
    total_cells, total_spots = cells * n_cell, spots * n_spot
    lines, peers = n_spot, n_cell // n_spot
    few_peers = peers <= 2
    s = lax.axis_index("spot")
    k = lax.axis_index("cell")
    z, y = k // peers, k % peers
    offset = s * spots

    def turn(value, d):
        pairs = [(i, (i // peers) * peers + (i % peers + d) % peers) for i in range(n_cell)]
        return lax.ppermute(value, "cell", pairs)

    order = [sorted(range(lines), key=lambda t: (-abs(t - a), abs(2 * t - lines + 1))) for a in range(lines)]
    far_line = entry(z, [order[a][0] for a in range(lines)])
    early = {}
    for d in range(1, peers if few_peers else 1):
        value = lax.dynamic_slice_in_dim(expression, ((y + d) % peers) * genes, genes, axis=1)
        left = n_spot - 1
        for bit in reversed(bits_of(n_spot)):
            pairs = [
                (j * n_cell + i, (j ^ bit) * n_cell + i)
                for i in range(n_cell)
                for j in range(n_spot)
                if (j ^ order[i // peers][0]) & left == 0
            ]
            got = lax.ppermute(value, ("spot", "cell"), pairs)
            value = jnp.where(((s ^ far_line) & left) == bit, got, value)
            left -= bit
        early[d] = value

    held = {0: expression}
    for bit in reversed(bits_of(n_spot)):
        pairs = [(i, i ^ bit) for i in range(n_spot)]
        held.update({m ^ bit: lax.ppermute(v, "spot", pairs) for m, v in list(held.items())})
    genes_all = jnp.concatenate(
        [choose(s, [(held[m], [i for i in range(n_spot) if i ^ m == j]) for m in held]) for j in range(n_spot)],
        axis=1,
    )
    (genes_all,) = apart(genes_all)

    def gene_block(block):
        return lax.dynamic_slice_in_dim(genes_all, block * genes, genes, axis=1)

    raised = jnp.exp(logits)
    local_sum = jnp.sum(raised, axis=0)
    (raised,) = apart(raised)
    column_sum = all_sum(local_sum, "cell", bits_of(n_cell)[::-1])
    mapping = raised / column_sum

    frame = spots + 2 * SIDE
    valid_all = spot_valid.astype(jnp.float32)
    nvalid = jnp.sum(valid_all)
    reach = SIDE + ROW + 1
    wide_valid = lax.dynamic_slice_in_dim(jnp.pad(valid_all, reach), offset, spots + 2 * reach)
    wide_slide = lax.dynamic_slice_in_dim(
        jnp.pad(slide_ids, reach, constant_values=-1), offset, spots + 2 * reach
    )
    up_spot = [(i, i + 1) for i in range(n_spot - 1)]
    down_spot = [(i + 1, i) for i in range(n_spot - 1)]

    def sides(tile):
        before = lax.ppermute(tile[:, -SIDE:], "spot", up_spot)
        after = lax.ppermute(tile[:, :SIDE], "spot", down_spot)
        return before, tile, after

    def framed(tile):
        return jnp.concatenate(sides(tile), axis=1)

    lists = framed(neighbours.T)
    spatial_wide = framed(spatial)
    spot_index = offset - SIDE + jnp.arange(frame, dtype=jnp.int32)
    inner = ROW + 1
    slide_frame = wide_slide[inner : inner + frame]
    valid_frame = wide_valid[inner : inner + frame]
    links = []
    for o in OFFSETS:
        listed = jnp.sum(((lists >= 0) & (lists == spot_index + o)).astype(jnp.float32), axis=0)
        there = wide_valid[inner + o : inner + o + frame] == 1.0
        same = wide_slide[inner + o : inner + o + frame] == slide_frame
        links.append(jnp.where(there & same, listed, 0.0))
    links = jnp.stack(links)
    counts = 1.0 + jnp.sum(links, axis=0)
    links, counts = apart(links, counts)
    valid_here = valid_frame[SIDE : SIDE + spots]
    slide_here = slide_frame[SIDE : SIDE + spots]
    members = (slide_here[None, :] == jnp.arange(SLIDES, dtype=jnp.int32)[:, None]).astype(jnp.float32)
    here, weighted = slice(SIDE, SIDE + spots), valid_here[None, :]
    early_sums = jnp.sum(members * (valid_here * density)[None, :], axis=1)
    early_sums = all_sum(early_sums, "spot", bits_of(n_spot))
    target = density / jnp.sum(members * early_sums[:, None], axis=0)
    frame_rows = jnp.stack([counts, valid_frame])
    gene_total = jnp.sum(genes_all, axis=1)
    ready = (links, frame_rows, spatial_wide, target, gene_total, nvalid)

    def part(block, columns=None):
        columns = gene_block(block) if columns is None else columns
        return lax.dot_general(columns, raised, (((0,), (0,)), ((), ())), precision=highest)

    def line_pairs(pairs):
        return [(a * peers + c, b * peers + c) for a, b in pairs for c in range(peers)]

    def along(near_value, far_value, up_from, down_from):
        hops = [(a, a + 1) for a in up_from] + [(a, a - 1) for a in down_from]
        links_of = [[hop for hop in hops if min(hop) % 2 == parity] for parity in range(2)]
        return [
            lax.ppermute(value, "cell", line_pairs(pairs)) if pairs else jnp.zeros_like(value)
            for value, pairs in zip((near_value, far_value), links_of)
        ]

    if few_peers:
        units = []
        for u in range(lines):
            to = entry(z, [order[a][u] for a in range(lines)])
            sent = [turn(part(to * peers + (y + d) % peers, None if u else early[d]), d) for d in range(1, peers)]
            (unit,) = apart(part(to * peers + y))
            for value in sent:
                unit = unit + value
            units.append(unit)

        def unit_for(target):
            wanted = [[] for _ in range(lines)]
            for a in range(lines):
                if 0 <= target(a) < lines:
                    wanted[order[a].index(target(a))].append(a)
            return choose(z, list(zip(units, wanted))) if any(wanted) else jnp.zeros_like(units[0])

        got_even = got_odd = None
        for p in range(lines - 1, 0, -1):
            even_value = unit_for(lambda a: a + p if a % 2 == 0 else a - p)
            odd_value = unit_for(lambda a: a - p if a % 2 == 0 else a + p)
            if got_even is not None:
                even_value, odd_value = even_value + got_odd, odd_value + got_even
            if p == 1:
                even_value, odd_value, *ready = apart(even_value, odd_value, *ready)
            got_even, got_odd = along(even_value, odd_value, range(0, lines - p), range(p, lines))
        predicted = unit_for(lambda a: a)
        if got_even is not None:
            predicted = predicted + got_even + got_odd
        column_sum, map_squares = apart(column_sum, jnp.sum(mapping * mapping * weighted))
        predicted = predicted / column_sum
    else:
        whole = lax.dot_general(genes_all, mapping, (((0,), (0,)), ((), ())), precision=highest)
        predicted = lax.psum_scatter(whole, "cell", scatter_dimension=0, tiled=True)
        map_squares = jnp.sum(mapping * mapping * weighted)

    links, frame_rows, spatial_wide, target, gene_total, nvalid = ready
    smoothed_wide, spot_sums, gene_sums = smooth_call(links, frame_rows, *sides(predicted), spatial_wide)
    gene_sums = all_sum(gene_sums[:, :4].T, "spot", bits_of(n_spot))
    spot_sums = all_sum(spot_sums, "cell", bits_of(n_cell))
    gene_inner, gene_own, gene_target, pred_squares = (gene_sums[i] for i in range(4))
    spot_inner, spot_own, spot_target, row_sums = (spot_sums[i] for i in range(4))
    row_sums = row_sums[here]
    gene_scale = lax.rsqrt((gene_own + epsilon) * (gene_target + epsilon))
    spot_scale = lax.rsqrt((spot_own + epsilon) * (spot_target + epsilon))
    cos_gene = gene_inner * gene_scale
    cos_spot = (spot_inner * spot_scale)[here]
    by_gene = total_cells * gene_scale
    by_spot = total_cells * total_spots / nvalid * spot_scale
    spread_in = (
        -valid_frame
        / counts
        * (
            (spatial_wide - (gene_inner / (gene_own + epsilon))[:, None] * smoothed_wide) * by_gene[:, None]
            + (spatial_wide - (spot_inner / (spot_own + epsilon))[None, :] * smoothed_wide) * by_spot[None, :]
        )
    )
    (spread_in,) = apart(spread_in)

    def shifted(value, o):
        return jnp.pad(value, ((0, 0), (ROW + 1, ROW + 1)))[:, ROW + 1 + o : ROW + 1 + o + frame]

    spread = spread_in
    for i, o in enumerate(OFFSETS):
        spread = spread + shifted(links[i] * spread_in, -o)
    grad_pred = spread[:, here]
    (grad_pred,) = apart(grad_pred)

    kl_known = valid_here * target * (jnp.log(target) - jnp.log(row_sums))
    spot_part = jnp.concatenate(
        [
            jnp.sum(valid_here * cos_spot)[None],
            jnp.sum(kl_known)[None],
            jnp.sum(members * (valid_here * target)[None, :], axis=1),
            jnp.sum(members * (valid_here * row_sums)[None, :], axis=1),
            map_squares[None],
        ]
    )
    spot_part = all_sum(spot_part, "spot", bits_of(n_spot))
    late = jnp.concatenate(
        [
            jnp.sum(predicted * grad_pred, axis=0),
            jnp.sum(pred_squares)[None],
            spot_part[2 + 2 * SLIDES :],
            jnp.sum(gene_own)[None],
            jnp.sum(cos_gene)[None],
        ]
    )
    late = all_sum(late, "cell", bits_of(n_cell))
    row_tot = spot_part[2 + SLIDES : 2 + 2 * SLIDES]
    slide_rows = jnp.sum(members * row_tot[:, None], axis=0)
    level = total_cells * total_spots * valid_here * (1.0 / slide_rows - target / row_sums)
    column_dot = late[:spots] + level * row_sums
    (mapping,) = apart(mapping)
    share = all_sum(jnp.sum(mapping * level[None, :], axis=1), "spot", bits_of(n_spot))

    pred_sq, map_sq, smooth_sq, cos_total = (late[spots + i] for i in range(4))
    gene_loss = 1.0 - cos_total / GENES
    spot_loss = 1.0 - spot_part[0] / nvalid
    density_loss = spot_part[1] + jnp.sum(jnp.where(row_tot > 0, spot_part[2 : 2 + SLIDES] * jnp.log(row_tot), 0.0))
    rms_weights = total_cells * jnp.sqrt(map_sq / (total_cells * nvalid))
    rms_pred = jnp.sqrt(pred_sq / (GENES * nvalid))
    rms_smooth = jnp.sqrt(smooth_sq / (GENES * nvalid))
    losses = (gene_loss, spot_loss, density_loss, rms_weights, rms_pred, rms_smooth)

    grad_map = None
    if few_peers:
        far = [sorted((t for t in range(lines)), key=lambda t: (abs(t - a), t)) for a in range(lines)]
        evens, odds = [grad_pred], [grad_pred]
        for p in range(1, lines):
            even, odd = along(odds[-1], evens[-1], range(p - 1, lines - 1), range(1, lines - p + 1))
            evens.append(even)
            odds.append(odd)
        slots = []
        for u in range(lines):
            options = [(grad_pred, [])] + [(v, []) for v in evens[1:]] + [(v, []) for v in odds[1:]]
            for a in range(lines):
                t = far[a][u]
                from_even = (a % 2 == 0) == (t > a)
                at = 0 if t == a else abs(a - t) + (0 if from_even else lines - 1)
                options[at][1].append(a)
            slots.append(choose(z, options))
            slots[u], *passed = apart(slots[u], *evens[1 : u + 1], *odds[1 : u + 1])
            evens[1 : u + 1], odds[1 : u + 1] = passed[:u], passed[u:]

        lines_at = [entry(z, [far[a][u] for a in range(lines)]) for u in range(lines)]
        waves = [[] for _ in range(lines + 1)]
        for u in range(lines):
            waves[u].append((u, 0, slots[u]))
            for d in range(1, peers):
                waves[u + 1].append((u, d, turn(slots[u], d)))
        kept = [None] * peers
        grad_expr = jnp.zeros((cells, gene_cols), jnp.float32)

        def placed(total, d):
            return lax.dynamic_update_slice_in_dim(total, kept[d] + share[:, None], ((y - d) % peers) * genes, axis=1)

        for w, wave in enumerate(waves):
            if w == lines:
                grad_expr = placed(grad_expr, 0)
                held_back = [kept[d] for d in range(1, peers)]
                blocks = [block for _, _, block in wave]
                *tied, losses = apart(grad_map, grad_expr, *held_back, *blocks, losses)
                grad_map, grad_expr = tied[:2]
                kept[1:] = tied[2 : 1 + peers]
                wave = [(u, d, block) for (u, d, _), block in zip(wave, tied[1 + peers :])]
            for u, d, block in wave:
                to = lines_at[u]
                names = to * peers + (y - d) % peers
                wide_grad = lax.dot_general(mapping, block, (((1,), (1,)), ((), ())), precision=highest)
                piece = jnp.dot(gene_block(names), block, precision=highest)
                for bit in bits_of(n_spot):
                    pairs = []
                    for i in range(n_cell):
                        t = far[i // peers][u]
                        for j in range(n_spot):
                            if (j ^ t) & (2 * bit - 1) == bit:
                                pairs.append((j * n_cell + i, (j ^ bit) * n_cell + i))
                    wide_grad = wide_grad + lax.ppermute(wide_grad, ("spot", "cell"), pairs)
                grad_map = piece if grad_map is None else grad_map + piece
                kept[d] = wide_grad if kept[d] is None else jnp.where(s == to, wide_grad, kept[d])
        for d in range(1, peers):
            grad_expr = placed(grad_expr, d)
    else:
        rows = lax.all_gather(grad_pred, "cell", axis=0, tiled=True)
        grad_map = jnp.dot(genes_all, rows, precision=highest)
        wide_grad = lax.dot_general(mapping, rows, (((1,), (1,)), ((), ())), precision=highest)
        grad_expr = lax.psum_scatter(wide_grad, "spot", scatter_dimension=1, tiled=True) + share[:, None]
    grad_logits = mapping * (grad_map + (gene_total[:, None] * level[None, :] - column_dot[None, :]))

    return (*losses[:3], grad_logits, grad_expr, *losses[3:])


def solution(mesh):
    placed = (
        P("cell", "spot"),
        P("cell", "spot"),
        P("cell", "spot"),
        P("spot"),
        P(),
        P(),
        P("spot", None),
    )
    step_map = jax.shard_map(
        step,
        mesh=mesh,
        in_specs=placed,
        out_specs=(P(), P(), P(), P("cell", "spot"), P("cell", "spot"), P(), P(), P()),
        check_vma=False,
    )
    if mesh.shape["cell"] > 2 * mesh.shape["spot"]:
        return step_map
    return step_map
```

```python
import jax
import jax.numpy as jnp
from jax import lax
from jax.experimental import pallas as pl
from jax.experimental.pallas import tpu as pltpu
from jax.sharding import PartitionSpec as P

GENES = 2048
ROW = 64
SLIDES = 3
SIDE = 2 * ROW
OFFSETS = (-ROW - 1, -ROW, -ROW + 1, -1, 1, ROW - 1, ROW, ROW + 1)

epsilon = 1e-06
highest = lax.Precision.HIGHEST


def apart(*values):
    return lax.optimization_barrier(values)


def bits_of(count):
    return [1 << b for b in range(count.bit_length() - 1)]


def all_sum(value, axis, bits):
    size = lax.axis_size(axis)
    for bit in bits:
        value = value + lax.ppermute(value, axis, [(i, i ^ bit) for i in range(size)])
    return value


def is_one_of(index, wanted):
    hit = index == wanted[0]
    for other in wanted[1:]:
        hit = hit | (index == other)
    return hit


def entry(index, values):
    picked = jnp.int32(values[0])
    for i, value in enumerate(values[1:], 1):
        picked = jnp.where(index == i, jnp.int32(value), picked)
    return picked


def choose(index, options):
    options = [o for o in options if o[1]]
    chosen = options[0][0]
    for value, wanted in options[1:]:
        chosen = jnp.where(is_one_of(index, wanted), value, chosen)
    return chosen


def smooth_kernel(links, rows, before, tile, after, spatial, smoothed, spot_sums, gene_sums):
    frame = spatial.shape[1]
    value = jnp.concatenate([before[...], tile[...], after[...]], axis=1)
    total = value
    for i, o in enumerate(OFFSETS):
        total = total + links[i : i + 1, :] * pltpu.roll(value, (-o) % frame, 1)
    smooth = total / rows[0:1, :]
    smoothed[...] = smooth
    there = spatial[...]
    inner, own = smooth * there, smooth * smooth

    @pl.when(pl.program_id(0) == 0)
    def _():
        spot_sums[...] = jnp.zeros_like(spot_sums)

    for i, part in enumerate((inner, own, there * there, value)):
        spot_sums[i : i + 1, :] += jnp.sum(part, axis=0, keepdims=True)
    here = slice(SIDE, frame - SIDE)
    valid = rows[1:2, here]
    lane = lax.broadcasted_iota(jnp.int32, gene_sums.shape, 1)
    sums = jnp.zeros(gene_sums.shape, jnp.float32)
    for i, part in enumerate((inner, own, there * there, value * value)):
        sums = jnp.where(lane == i, jnp.sum(valid * part[:, here], axis=1, keepdims=True), sums)
    gene_sums[...] = sums


def smooth_call(links, rows, before, tile, after, spatial):
    genes, frame = spatial.shape
    step = min(32, genes)
    whole = lambda a: pl.BlockSpec(a.shape, lambda i: (0, 0))
    some = lambda width: pl.BlockSpec((step, width), lambda i: (i, 0))
    return pl.pallas_call(
        smooth_kernel,
        grid=(genes // step,),
        in_specs=[whole(links), whole(rows), some(SIDE), some(tile.shape[1]), some(SIDE), some(frame)],
        out_specs=[some(frame), pl.BlockSpec((4, frame), lambda i: (0, 0)), some(128)],
        out_shape=[
            jax.ShapeDtypeStruct((genes, frame), jnp.float32),
            jax.ShapeDtypeStruct((4, frame), jnp.float32),
            jax.ShapeDtypeStruct((genes, 128), jnp.float32),
        ],
        name="smooth",
    )(links, rows, before, tile, after, spatial)


def step(logits, expression, spatial, density, slide_ids, spot_valid, neighbours):
    cells, spots = logits.shape
    genes = spatial.shape[0]
    gene_cols = expression.shape[1]
    n_spot, n_cell = lax.axis_size("spot"), lax.axis_size("cell")
    total_cells, total_spots = cells * n_cell, spots * n_spot
    lines, peers = n_spot, n_cell // n_spot
    few_peers = peers <= 2
    s = lax.axis_index("spot")
    k = lax.axis_index("cell")
    z, y = k // peers, k % peers
    offset = s * spots

    def turn(value, d):
        pairs = [(i, (i // peers) * peers + (i % peers + d) % peers) for i in range(n_cell)]
        return lax.ppermute(value, "cell", pairs)

    order = [sorted(range(lines), key=lambda t: (-abs(t - a), abs(2 * t - lines + 1))) for a in range(lines)]
    far_line = entry(z, [order[a][0] for a in range(lines)])
    early = {}
    for d in range(1, peers if few_peers else 1):
        value = lax.dynamic_slice_in_dim(expression, ((y + d) % peers) * genes, genes, axis=1)
        left = n_spot - 1
        for bit in reversed(bits_of(n_spot)):
            pairs = [
                (j * n_cell + i, (j ^ bit) * n_cell + i)
                for i in range(n_cell)
                for j in range(n_spot)
                if (j ^ order[i // peers][0]) & left == 0
            ]
            got = lax.ppermute(value, ("spot", "cell"), pairs)
            value = jnp.where(((s ^ far_line) & left) == bit, got, value)
            left -= bit
        early[d] = value

    held = {0: expression}
    for bit in reversed(bits_of(n_spot)):
        pairs = [(i, i ^ bit) for i in range(n_spot)]
        held.update({m ^ bit: lax.ppermute(v, "spot", pairs) for m, v in list(held.items())})
    genes_all = jnp.concatenate(
        [choose(s, [(held[m], [i for i in range(n_spot) if i ^ m == j]) for m in held]) for j in range(n_spot)],
        axis=1,
    )
    (genes_all,) = apart(genes_all)

    def gene_block(block):
        return lax.dynamic_slice_in_dim(genes_all, block * genes, genes, axis=1)

    raised = jnp.exp(logits)
    local_sum = jnp.sum(raised, axis=0)
    (raised,) = apart(raised)
    column_sum = all_sum(local_sum, "cell", bits_of(n_cell)[::-1])
    mapping = raised / column_sum

    frame = spots + 2 * SIDE
    valid_all = spot_valid.astype(jnp.float32)
    nvalid = jnp.sum(valid_all)
    reach = SIDE + ROW + 1
    wide_valid = lax.dynamic_slice_in_dim(jnp.pad(valid_all, reach), offset, spots + 2 * reach)
    wide_slide = lax.dynamic_slice_in_dim(
        jnp.pad(slide_ids, reach, constant_values=-1), offset, spots + 2 * reach
    )
    up_spot = [(i, i + 1) for i in range(n_spot - 1)]
    down_spot = [(i + 1, i) for i in range(n_spot - 1)]

    def sides(tile):
        before = lax.ppermute(tile[:, -SIDE:], "spot", up_spot)
        after = lax.ppermute(tile[:, :SIDE], "spot", down_spot)
        return before, tile, after

    def framed(tile):
        return jnp.concatenate(sides(tile), axis=1)

    lists = framed(neighbours.T)
    spatial_wide = framed(spatial)
    spot_index = offset - SIDE + jnp.arange(frame, dtype=jnp.int32)
    inner = ROW + 1
    slide_frame = wide_slide[inner : inner + frame]
    valid_frame = wide_valid[inner : inner + frame]
    links = []
    for o in OFFSETS:
        listed = jnp.sum(((lists >= 0) & (lists == spot_index + o)).astype(jnp.float32), axis=0)
        there = wide_valid[inner + o : inner + o + frame] == 1.0
        same = wide_slide[inner + o : inner + o + frame] == slide_frame
        links.append(jnp.where(there & same, listed, 0.0))
    links = jnp.stack(links)
    counts = 1.0 + jnp.sum(links, axis=0)
    links, counts = apart(links, counts)
    valid_here = valid_frame[SIDE : SIDE + spots]
    slide_here = slide_frame[SIDE : SIDE + spots]
    members = (slide_here[None, :] == jnp.arange(SLIDES, dtype=jnp.int32)[:, None]).astype(jnp.float32)
    here, weighted = slice(SIDE, SIDE + spots), valid_here[None, :]
    early_sums = jnp.sum(members * (valid_here * density)[None, :], axis=1)
    early_sums = all_sum(early_sums, "spot", bits_of(n_spot))
    target = density / jnp.sum(members * early_sums[:, None], axis=0)
    frame_rows = jnp.stack([counts, valid_frame])
    gene_total = jnp.sum(genes_all, axis=1)
    ready = (links, frame_rows, spatial_wide, target, gene_total, nvalid)

    def part(block, columns=None):
        columns = gene_block(block) if columns is None else columns
        return lax.dot_general(columns, raised, (((0,), (0,)), ((), ())), precision=highest)

    def line_pairs(pairs):
        return [(a * peers + c, b * peers + c) for a, b in pairs for c in range(peers)]

    def along(near_value, far_value, up_from, down_from):
        hops = [(a, a + 1) for a in up_from] + [(a, a - 1) for a in down_from]
        links_of = [[hop for hop in hops if min(hop) % 2 == parity] for parity in range(2)]
        return [
            lax.ppermute(value, "cell", line_pairs(pairs)) if pairs else jnp.zeros_like(value)
            for value, pairs in zip((near_value, far_value), links_of)
        ]

    if few_peers:
        units = []
        for u in range(lines):
            to = entry(z, [order[a][u] for a in range(lines)])
            sent = [turn(part(to * peers + (y + d) % peers, None if u else early[d]), d) for d in range(1, peers)]
            (unit,) = apart(part(to * peers + y))
            for value in sent:
                unit = unit + value
            units.append(unit)

        def unit_for(target):
            wanted = [[] for _ in range(lines)]
            for a in range(lines):
                if 0 <= target(a) < lines:
                    wanted[order[a].index(target(a))].append(a)
            return choose(z, list(zip(units, wanted))) if any(wanted) else jnp.zeros_like(units[0])

        got_even = got_odd = None
        for p in range(lines - 1, 0, -1):
            even_value = unit_for(lambda a: a + p if a % 2 == 0 else a - p)
            odd_value = unit_for(lambda a: a - p if a % 2 == 0 else a + p)
            if got_even is not None:
                even_value, odd_value = even_value + got_odd, odd_value + got_even
            if p == 1:
                even_value, odd_value, *ready = apart(even_value, odd_value, *ready)
            got_even, got_odd = along(even_value, odd_value, range(0, lines - p), range(p, lines))
        predicted = unit_for(lambda a: a)
        if got_even is not None:
            predicted = predicted + got_even + got_odd
        predicted = predicted / column_sum
    else:
        whole = lax.dot_general(genes_all, mapping, (((0,), (0,)), ((), ())), precision=highest)
        predicted = lax.psum_scatter(whole, "cell", scatter_dimension=0, tiled=True)

    links, frame_rows, spatial_wide, target, gene_total, nvalid = ready
    smoothed_wide, spot_sums, gene_sums = smooth_call(links, frame_rows, *sides(predicted), spatial_wide)
    gene_sums = all_sum(gene_sums[:, :4].T, "spot", bits_of(n_spot))
    spot_sums = all_sum(spot_sums, "cell", bits_of(n_cell))
    gene_inner, gene_own, gene_target, pred_squares = (gene_sums[i] for i in range(4))
    spot_inner, spot_own, spot_target, row_sums = (spot_sums[i] for i in range(4))
    row_sums = row_sums[here]
    gene_scale = lax.rsqrt((gene_own + epsilon) * (gene_target + epsilon))
    spot_scale = lax.rsqrt((spot_own + epsilon) * (spot_target + epsilon))
    cos_gene = gene_inner * gene_scale
    cos_spot = (spot_inner * spot_scale)[here]
    by_gene = total_cells * gene_scale
    by_spot = total_cells * total_spots / nvalid * spot_scale
    spread_in = (
        -valid_frame
        / counts
        * (
            (spatial_wide - (gene_inner / (gene_own + epsilon))[:, None] * smoothed_wide) * by_gene[:, None]
            + (spatial_wide - (spot_inner / (spot_own + epsilon))[None, :] * smoothed_wide) * by_spot[None, :]
        )
    )
    (spread_in,) = apart(spread_in)

    def shifted(value, o):
        return jnp.pad(value, ((0, 0), (ROW + 1, ROW + 1)))[:, ROW + 1 + o : ROW + 1 + o + frame]

    spread = spread_in
    for i, o in enumerate(OFFSETS):
        spread = spread + shifted(links[i] * spread_in, -o)
    grad_pred = spread[:, here]
    (grad_pred,) = apart(grad_pred)

    kl_known = valid_here * target * (jnp.log(target) - jnp.log(row_sums))
    spot_part = jnp.concatenate(
        [
            jnp.sum(valid_here * cos_spot)[None],
            jnp.sum(kl_known)[None],
            jnp.sum(members * (valid_here * target)[None, :], axis=1),
            jnp.sum(members * (valid_here * row_sums)[None, :], axis=1),
            jnp.sum(mapping * mapping * weighted)[None],
        ]
    )
    spot_part = all_sum(spot_part, "spot", bits_of(n_spot))
    late = jnp.concatenate(
        [
            jnp.sum(predicted * grad_pred, axis=0),
            jnp.sum(pred_squares)[None],
            spot_part[2 + 2 * SLIDES :],
            jnp.sum(gene_own)[None],
            jnp.sum(cos_gene)[None],
        ]
    )
    late = all_sum(late, "cell", bits_of(n_cell))
    row_tot = spot_part[2 + SLIDES : 2 + 2 * SLIDES]
    slide_rows = jnp.sum(members * row_tot[:, None], axis=0)
    level = total_cells * total_spots * valid_here * (1.0 / slide_rows - target / row_sums)
    column_dot = late[:spots] + level * row_sums
    (mapping,) = apart(mapping)
    share = all_sum(jnp.sum(mapping * level[None, :], axis=1), "spot", bits_of(n_spot))

    pred_sq, map_sq, smooth_sq, cos_total = (late[spots + i] for i in range(4))
    gene_loss = 1.0 - cos_total / GENES
    spot_loss = 1.0 - spot_part[0] / nvalid
    density_loss = spot_part[1] + jnp.sum(jnp.where(row_tot > 0, spot_part[2 : 2 + SLIDES] * jnp.log(row_tot), 0.0))
    rms_weights = total_cells * jnp.sqrt(map_sq / (total_cells * nvalid))
    rms_pred = jnp.sqrt(pred_sq / (GENES * nvalid))
    rms_smooth = jnp.sqrt(smooth_sq / (GENES * nvalid))
    losses = (gene_loss, spot_loss, density_loss, rms_weights, rms_pred, rms_smooth)

    grad_map = None
    if few_peers:
        far = [sorted((t for t in range(lines)), key=lambda t: (abs(t - a), t)) for a in range(lines)]
        evens, odds = [grad_pred], [grad_pred]
        for p in range(1, lines):
            even, odd = along(odds[-1], evens[-1], range(p - 1, lines - 1), range(1, lines - p + 1))
            evens.append(even)
            odds.append(odd)
        slots = []
        for u in range(lines):
            options = [(grad_pred, [])] + [(v, []) for v in evens[1:]] + [(v, []) for v in odds[1:]]
            for a in range(lines):
                t = far[a][u]
                from_even = (a % 2 == 0) == (t > a)
                at = 0 if t == a else abs(a - t) + (0 if from_even else lines - 1)
                options[at][1].append(a)
            slots.append(choose(z, options))
            slots[u], *passed = apart(slots[u], *evens[1 : u + 1], *odds[1 : u + 1])
            evens[1 : u + 1], odds[1 : u + 1] = passed[:u], passed[u:]

        lines_at = [entry(z, [far[a][u] for a in range(lines)]) for u in range(lines)]

        def to_line(value, u):
            for bit in bits_of(n_spot):
                pairs = []
                for i in range(n_cell):
                    t = far[i // peers][u]
                    for j in range(n_spot):
                        if (j ^ t) & (2 * bit - 1) == bit:
                            pairs.append((j * n_cell + i, (j ^ bit) * n_cell + i))
                value = value + lax.ppermute(value, ("spot", "cell"), pairs)
            return value

        def by_mapping(rows):
            return lax.dot_general(mapping, rows, (((1,), (1,)), ((), ())), precision=highest)

        def added(piece):
            return piece if grad_map is None else grad_map + piece

        grad_expr = jnp.zeros((cells, gene_cols), jnp.float32)
        for u in range(lines - 1):
            blocks = [slots[u]] + [turn(slots[u], d) for d in range(1, peers)]
            rows = jnp.concatenate(
                [
                    choose(y, [(b, [c for c in range(peers) if (c - d) % peers == q]) for d, b in enumerate(blocks)])
                    for q in range(peers)
                ],
                axis=0,
            )
            (rows,) = apart(rows)
            columns = lax.dynamic_slice_in_dim(genes_all, lines_at[u] * gene_cols, gene_cols, axis=1)
            wide_grad = by_mapping(rows)
            piece = jnp.dot(columns, rows, precision=highest)
            wide_grad = to_line(wide_grad, u)
            grad_map = added(piece)
            grad_expr = jnp.where(s == lines_at[u], wide_grad, grad_expr)
        u = lines - 1
        mine = s == lines_at[u]

        def with_last(d, block):
            at = ((y - d) % peers) * genes
            wide_grad = to_line(by_mapping(block), u)
            value = jnp.where(mine, wide_grad, lax.dynamic_slice_in_dim(grad_expr, at, genes, axis=1))
            piece = jnp.dot(gene_block(lines_at[u] * peers + (y - d) % peers), block, precision=highest)
            return lax.dynamic_update_slice_in_dim(grad_expr, value + share[:, None], at, axis=1), added(piece)

        grad_expr, grad_map = with_last(0, slots[u])
        for d in range(1, peers):
            block = turn(slots[u], d)
            grad_map, block, losses = apart(grad_map, block, losses)
            grad_expr, grad_map = with_last(d, block)
    else:
        rows = lax.all_gather(grad_pred, "cell", axis=0, tiled=True)
        grad_map = jnp.dot(genes_all, rows, precision=highest)
        wide_grad = lax.dot_general(mapping, rows, (((1,), (1,)), ((), ())), precision=highest)
        grad_expr = lax.psum_scatter(wide_grad, "spot", scatter_dimension=1, tiled=True) + share[:, None]
    grad_logits = mapping * (grad_map + (gene_total[:, None] * level[None, :] - column_dot[None, :]))

    return (*losses[:3], grad_logits, grad_expr, *losses[3:])


def solution(mesh):
    placed = (
        P("cell", "spot"),
        P("cell", "spot"),
        P("cell", "spot"),
        P("spot"),
        P(),
        P(),
        P("spot", None),
    )
    step_map = jax.shard_map(
        step,
        mesh=mesh,
        in_specs=placed,
        out_specs=(P(), P(), P(), P("cell", "spot"), P("cell", "spot"), P(), P(), P()),
        check_vma=False,
    )
    if mesh.shape["cell"] > 2 * mesh.shape["spot"]:
        return step_map
    return step_map
```
